128 devices in a mesh: outer: 2 (over core), nodes: 64 (over z, y, x).
Axes of the slice: x: 4, y: 4, z: 4, core: 2. Of those that a mesh axis runs over, the one named last changes fastest.
Arguments:
- features: bfloat16 [65536, 512], P(('outer', 'nodes')), may hold values from -6 to 6
- w_query: bfloat16 [512, 512], replicated, may hold values from -0.25 to 0.25
- w_key: bfloat16 [512, 512], replicated, may hold values from -0.75 to 0.75
- w_value: bfloat16 [512, 512], replicated, may hold values from -0.25 to 0.25
- bases: bfloat16 [2, 512, 512], replicated, may hold values from -0.09375 to 0.09375
- rel_coef: float32 [8, 2], replicated, may hold values from -4 to 4
- send_rows: int32 [128, 64, 32], P(('outer', 'nodes')), may hold values from 0 to 511
- tile_src: int32 [128, 8, 4, 128], P(('outer', 'nodes')), may hold values from 0 to 2559, as said below
- tile_dst: int32 [128, 8, 4, 128], P(('outer', 'nodes')), may hold values from 0 to 127
- tile_count: int32 [128, 8, 4], P(('outer', 'nodes')), may hold values from 1 to 128, as said below
- cotangent: float32 [65536, 512], P(('outer', 'nodes')), may hold values from -6 to 6
Outputs:
- layer_out: float32 [65536, 512], P(('outer', 'nodes'))
- grad_x: float32 [65536, 512], P(('outer', 'nodes'))
- query_grad: float32 [512, 512], replicated
- key_grad: float32 [512, 512], replicated
- value_grad: float32 [512, 512], replicated
- bases_grad: float32 [2, 512, 512], replicated
- coef_grad: float32 [8, 2], replicated
The draws below stay inside these ranges and needn't reach their ends.
Inputs may be any that keep to these rules, and one draw needn't show every extreme that they name: `send_rows`: row indices into the sending device's own 512 rows. `tile_src`: rows of the device's table (its own 512 rows, then 32 slots from each node position of its group in order). Edges read only slots of other devices of the group, and of each sender only its first slots, as many as that sender fills for this device, between 1 and 32. The first tile_count slots of a tile hold its edges. Every device has a tile with all 128 slots used.
All inputs are finite; a program needn't handle non-finite values.
Results may differ from the reference program's by a relative error of at most 0.0041.
Values may be sent and summed in bfloat16 or wider, within the bound.
A program may use at most 128 MiB of HBM per device.

```python
import jax
import jax.numpy as jnp
from jax import lax

D = 512
HEADS = 8
HEAD_DIM = 64
REL = 8
BASES = 2
TILE = 128
EDGE_CAP = 128
SEND_CAP = 32
NODE_DEV = 512
NODES = 65536
TILES = 4
N_NODES = 64
DEVICES = 128


def draw_tile_src(key, part):
    array_shape = (DEVICES, REL, TILES, EDGE_CAP)
    filled = jax.random.randint(jax.random.fold_in(key, 5), (DEVICES, N_NODES), 1, SEND_CAP + 1)
    sender_pos = (jnp.arange(DEVICES, dtype=jnp.int32) % N_NODES)[:, None]
    receiver_pos = jnp.arange(N_NODES, dtype=jnp.int32)[None, :]
    forced_full = (sender_pos == N_NODES - 1) & (receiver_pos == 0)
    filled = jnp.where(forced_full, SEND_CAP, filled)
    device = jnp.arange(DEVICES, dtype=jnp.int32).reshape(DEVICES, 1, 1, 1)
    group_index = device // N_NODES
    position = device % N_NODES
    subkeys = jax.random.split(jax.random.fold_in(key, 11), 4)
    local_row = jax.random.randint(subkeys[0], array_shape, 0, NODE_DEV)
    hop_count = jax.random.randint(subkeys[1], array_shape, 0, N_NODES - 1)
    peer_node = (position + 1 + hop_count) % N_NODES
    sender = group_index * N_NODES + peer_node
    filled_here = filled[sender, position]
    slot_index = jax.random.randint(subkeys[2], array_shape, 0, 1 << 20) % filled_here
    halo_row = NODE_DEV + peer_node * SEND_CAP + slot_index
    remote = jax.random.randint(subkeys[3], array_shape, 0, 2) == 1
    result = jnp.where(remote, halo_row, local_row).astype(jnp.int32)
    result = result.at[0, 0, 0, 0].set(NODE_DEV + N_NODES * SEND_CAP - 1)
    result = result.at[0, 0, 0, 1].set(0)
    return result.astype(jnp.int32)


def draw_tile_count(key, part):
    subkeys = jax.random.split(jax.random.fold_in(key, 23), 3)
    weight_level = jax.random.randint(subkeys[0], (DEVICES, REL, 1), 1, 5)
    ceiling = EDGE_CAP * weight_level // 4
    drawn = jax.random.randint(subkeys[1], (DEVICES, REL, TILES), 0, 1 << 20) % (ceiling // 2 + 1)
    counts = ceiling - drawn
    chosen = jax.random.randint(subkeys[2], (DEVICES, 1), 0, REL * TILES)
    full_tile = (jnp.arange(REL * TILES, dtype=jnp.int32)[None, :] == chosen).reshape(DEVICES, REL, TILES)
    return jnp.where(full_tile, EDGE_CAP, counts).astype(jnp.int32)


def set_ends(entries, rng, low, top_value):
    longest = entries.shape.index(max(entries.shape))
    spots = []
    for shift in (0, 1):
        where = [jax.random.randint(jax.random.fold_in(rng, axis), (), 0, length) for axis, length in enumerate(entries.shape)]
        where[longest] = (where[longest] + shift) % entries.shape[longest]
        spots.append(tuple(where))
    return entries.at[spots[0]].set(low).at[spots[1]].set(top_value)


def steps_of(rng, extent, cuts, least, high):
    loudness, own = 1.0, jax.random.fold_in(rng, 6)
    for axis_at, parts in cuts:
        heights = jnp.exp(jax.random.uniform(jax.random.fold_in(own, axis_at), (parts,), jnp.float32, least / len(cuts), high / len(cuts)))
        loudness = loudness * jnp.repeat(heights, extent[axis_at] // parts).reshape([-1 if axis == axis_at else 1 for axis in range(len(extent))])
    return loudness


def scatter_about(key, extent, deviation, most, cuts=(), held_as=jnp.bfloat16):
    values = jax.random.normal(key, extent, jnp.float32) * deviation
    if len(cuts) > 0:
        values = steps_of(key, extent, cuts, -0.22, 0.18) * values
    return jnp.clip(values, min=-most, max=most).astype(held_as)


def setup_inputs(seed: int = 0) -> dict:
    keys = jax.random.split(jax.random.key(seed), 12)
    features = scatter_about(keys[0], (NODES, D), 1.0, 6.0, ((0, 128),))
    w_query = scatter_about(keys[1], (D, D), D ** -0.5, 0.25)
    w_key = scatter_about(keys[2], (D, D), (D // 8) ** -0.5, 0.75)
    w_value = scatter_about(keys[3], (D, D), D ** -0.5, 0.25)
    bases = scatter_about(keys[4], (BASES, D, D), (REL * D) ** -0.5, 0.09375)
    rel_coef = scatter_about(keys[5], (REL, BASES), 1.0, 4.0, (), jnp.float32)
    send_rows = set_ends(jax.random.randint(keys[6], (DEVICES, N_NODES, SEND_CAP), 0, NODE_DEV), jax.random.fold_in(keys[6], 1), 0, NODE_DEV - 1).astype(jnp.int32)
    tile_src = draw_tile_src(jax.random.fold_in(keys[11], 71), 0)
    tile_dst = set_ends(jax.random.randint(keys[8], (DEVICES, REL, TILES, EDGE_CAP), 0, TILE), jax.random.fold_in(keys[8], 1), 0, TILE - 1).astype(jnp.int32)
    tile_count = draw_tile_count(jax.random.fold_in(keys[11], 71), 0)
    cotangent = scatter_about(keys[10], (NODES, D), 1.0, 6.0, ((0, 128),), jnp.float32)
    return dict(features=features, w_query=w_query, w_key=w_key, w_value=w_value, bases=bases, rel_coef=rel_coef, send_rows=send_rows, tile_src=tile_src, tile_dst=tile_dst, tile_count=tile_count, cotangent=cotangent)


precise = lax.Precision.HIGHEST


def reference(features, w_query, w_key, w_value, bases, rel_coef, send_rows, tile_src, tile_dst, tile_count, cotangent):
    table_rows = NODE_DEV + N_NODES * SEND_CAP
    norm_scale = 1.0 / (NODES ** 0.5)
    w_all = jnp.concatenate([w_query, w_key, w_value], axis=1)
    projected = jnp.dot(features, w_all, preferred_element_type=jnp.float32)
    exp_query = jnp.exp(projected[:, :D]).reshape(NODES, HEADS, HEAD_DIM)
    exp_key = jnp.exp(projected[:, D:2 * D]).reshape(NODES, HEADS, HEAD_DIM)
    values = projected[:, 2 * D:].reshape(NODES, HEADS, HEAD_DIM)
    kv_sum = jnp.einsum('ihd,ihe->hde', exp_key, values, precision=precise)
    ks_sum = jnp.sum(exp_key, axis=0)
    normalizer = jnp.einsum('ihd,hd->ih', exp_query, ks_sum, precision=precise)
    attended = jnp.einsum('ihd,hde->ihe', exp_query, kv_sum, precision=precise) / normalizer[:, :, None]
    cot_half = cotangent.astype(jnp.bfloat16)
    bases_wide = bases.astype(jnp.float32)

    def device_step(carry, device):
        graph_grad, bases_acc, coef_acc = carry
        group_index = device // N_NODES
        position = device % N_NODES
        own_rows = lax.dynamic_slice_in_dim(features, device * NODE_DEV, NODE_DEV, 0)
        senders = group_index * N_NODES + jnp.arange(N_NODES, dtype=jnp.int32)
        picks = send_rows[senders, position, :]
        global_rows = (senders[:, None] * NODE_DEV + picks).reshape(-1).astype(jnp.int32)
        halo_table = jnp.concatenate([own_rows, features[global_rows]], axis=0)
        sources = tile_src[device].reshape(-1)
        targets = tile_dst[device]
        counts = tile_count[device]
        live_mask = jnp.arange(EDGE_CAP, dtype=jnp.int32)[None, None, :] < counts[:, :, None]
        segment = (jnp.arange(REL, dtype=jnp.int32)[:, None, None] * NODE_DEV
                   + jnp.arange(TILES, dtype=jnp.int32)[None, :, None] * TILE + targets).reshape(-1).astype(jnp.int32)
        live_wide = live_mask.reshape(-1).astype(jnp.float32)
        gathered = halo_table[sources].astype(jnp.float32) * live_wide[:, None]
        row_sums = jax.ops.segment_sum(gathered, segment, num_segments=REL * NODE_DEV).reshape(REL, NODE_DEV, D)
        degree = jnp.maximum(jax.ops.segment_sum(live_wide, segment, num_segments=REL * NODE_DEV), 1.0).reshape(REL, NODE_DEV)
        aggregate = row_sums / degree[:, :, None]
        basis_in = jnp.einsum('rb,rmd->bmd', rel_coef, aggregate, precision=precise).astype(jnp.bfloat16)
        basis_wide = basis_in.astype(jnp.float32)
        conv_out = jnp.einsum('bmd,bde->me', basis_wide, bases_wide, precision=precise)
        cot_dev = lax.dynamic_slice_in_dim(cot_half, device * NODE_DEV, NODE_DEV, 0).astype(jnp.float32)
        basis_grad = jnp.einsum('me,bde->bmd', cot_dev, bases_wide, precision=precise)
        bases_acc = bases_acc + jnp.einsum('bmd,me->bde', basis_wide, cot_dev, precision=precise)
        coef_acc = coef_acc + jnp.einsum('rmd,bmd->rb', aggregate, basis_grad, precision=precise)
        agg_grad = jnp.einsum('rb,bmd->rmd', rel_coef, basis_grad, precision=precise) / degree[:, :, None]
        moved = agg_grad.reshape(-1, D)[segment] * live_wide[:, None]
        table_grad = jax.ops.segment_sum(moved, sources, num_segments=table_rows)
        own_grad = lax.dynamic_slice_in_dim(graph_grad, device * NODE_DEV, NODE_DEV, 0) + table_grad[:NODE_DEV]
        graph_grad = lax.dynamic_update_slice_in_dim(graph_grad, own_grad, device * NODE_DEV, 0)
        graph_grad = graph_grad.at[global_rows].add(table_grad[NODE_DEV:])
        return (graph_grad, bases_acc, coef_acc), conv_out

    start_carry = (jnp.zeros((NODES, D), jnp.float32), jnp.zeros((BASES, D, D), jnp.float32),
                   jnp.zeros((REL, BASES), jnp.float32))
    carry, conv_all = lax.scan(device_step, start_carry, jnp.arange(DEVICES, dtype=jnp.int32))
    graph_grad, bases_acc, coef_acc = carry
    layer_out = attended.reshape(NODES, D) + conv_all.reshape(NODES, D)

    grad_heads = cotangent.reshape(NODES, HEADS, HEAD_DIM)
    num_grad = grad_heads / normalizer[:, :, None]
    den_grad = -jnp.sum(grad_heads * attended, axis=2) / normalizer
    query_side = jnp.einsum('ihe,hde->ihd', num_grad, kv_sum, precision=precise) + den_grad[:, :, None] * ks_sum[None]
    dkv_sum = jnp.einsum('ihd,ihe->hde', exp_query, num_grad, precision=precise)
    dks_sum = jnp.einsum('ihd,ih->hd', exp_query, den_grad, precision=precise)
    key_side = jnp.einsum('ihe,hde->ihd', values, dkv_sum, precision=precise) + dks_sum[None]
    value_side = jnp.einsum('ihd,hde->ihe', exp_key, dkv_sum, precision=precise)
    proj_grad = jnp.concatenate([(query_side * exp_query).reshape(NODES, D), (key_side * exp_key).reshape(NODES, D),
                                 value_side.reshape(NODES, D)], axis=1).astype(jnp.bfloat16)
    grad_x = jnp.dot(proj_grad, w_all.T, preferred_element_type=jnp.float32) + graph_grad
    weight_all = jnp.dot(features.T, proj_grad, preferred_element_type=jnp.float32) * norm_scale
    query_grad = weight_all[:, :D]
    key_grad = weight_all[:, D:2 * D]
    value_grad = weight_all[:, 2 * D:]
    return (layer_out, grad_x, query_grad, key_grad, value_grad, bases_acc * norm_scale, coef_acc * norm_scale)
```

```python
import math

import jax
import jax.numpy as jnp
from jax import lax
from jax.sharding import PartitionSpec as P

HEADS = 8
HEAD_DIM = 64
TILE = 128


precise = lax.Precision.HIGHEST
three_pass = lax.Precision.HIGH


def per_device(
    features,
    w_query,
    w_key,
    w_value,
    bases,
    rel_coef,
    send_rows,
    tile_src,
    tile_dst,
    tile_count,
    cotangent,
):
    node_rows, feat_width = features.shape
    peer_count = lax.axis_size("nodes")
    total_nodes = node_rows * peer_count * lax.axis_size("outer")
    norm_scale = 1.0 / math.sqrt(total_nodes)
    basis_count = bases.shape[0]
    send_list = send_rows[0]
    peer_slots = send_list.shape[1]
    send_flat = send_list.reshape(-1)
    pick = (send_flat[:, None] == jnp.arange(node_rows)[None, :]).astype(jnp.bfloat16)
    outgoing = jnp.dot(pick, features, preferred_element_type=jnp.float32).astype(jnp.bfloat16)
    outgoing = outgoing.reshape(peer_count, peer_slots, feat_width)
    incoming = lax.all_to_all(outgoing, "nodes", split_axis=0, concat_axis=0, tiled=True)
    halo_table = jnp.concatenate([features, incoming.reshape(-1, feat_width)], axis=0)
    table_rows = halo_table.shape[0]

    w_all = jnp.concatenate([w_query, w_key, w_value], axis=1)
    projected = jnp.dot(features, w_all, preferred_element_type=jnp.float32)
    exp_query = jnp.exp(projected[:, :feat_width]).reshape(node_rows, HEADS, HEAD_DIM)
    exp_key = jnp.exp(projected[:, feat_width : 2 * feat_width]).reshape(node_rows, HEADS, HEAD_DIM)
    values = projected[:, 2 * feat_width :].reshape(node_rows, HEADS, HEAD_DIM)
    kv_part = jnp.einsum("ihd,ihe->hde", exp_key, values, precision=precise)
    ks_part = jnp.sum(exp_key, axis=0)
    kv_size = kv_part.size
    summary = lax.psum(
        jnp.concatenate([kv_part.reshape(-1), ks_part.reshape(-1)]), ("outer", "nodes")
    )
    kv_sum = summary[:kv_size].reshape(kv_part.shape)
    ks_sum = summary[kv_size:].reshape(ks_part.shape)

    src_all = tile_src[0]
    dst_all = tile_dst[0]
    count_all = tile_count[0]
    rel_count, tile_count_n, slot_count = src_all.shape
    live = jnp.arange(slot_count)[None, None, :] < count_all[:, :, None]
    dst_hot = (dst_all[..., None] == jnp.arange(TILE)).astype(jnp.bfloat16) * live[
        ..., None
    ].astype(jnp.bfloat16)
    src_hot = (src_all[..., None] == jnp.arange(table_rows)).astype(jnp.bfloat16)
    edge_counts = jnp.einsum(
        "rtej,rten->rtjn", dst_hot, src_hot, preferred_element_type=jnp.float32
    ).astype(jnp.bfloat16)
    degree = jnp.maximum(jnp.sum(dst_hot.astype(jnp.float32), axis=2), 1.0)
    row_sums = jnp.einsum(
        "rtjn,nd->rtjd", edge_counts, halo_table, preferred_element_type=jnp.float32
    )
    aggregate = (row_sums / degree[..., None]).reshape(rel_count, node_rows, feat_width)
    basis_in = jnp.einsum("rb,rmd->bmd", rel_coef, aggregate, precision=precise).astype(
        jnp.bfloat16
    )
    conv_out = jnp.einsum("bmd,bde->me", basis_in, bases, preferred_element_type=jnp.float32)
    normalizer = jnp.einsum("ihd,hd->ih", exp_query, ks_sum, precision=precise)
    attended = (
        jnp.einsum("ihd,hde->ihe", exp_query, kv_sum, precision=precise) / normalizer[:, :, None]
    )
    layer_out = attended.reshape(node_rows, feat_width) + conv_out
    cot_half = cotangent.astype(jnp.bfloat16)
    basis_grad = jnp.einsum("me,bde->bmd", cot_half, bases, preferred_element_type=jnp.float32)
    coef_part = jnp.einsum("rmd,bmd->rb", aggregate, basis_grad, precision=precise)
    weight_rb = rel_coef[:, :, None, None] / degree[:, None, :, :]
    basis_hot = jnp.einsum(
        "rbtj,rtjn->btjn", weight_rb, edge_counts.astype(jnp.float32), precision=precise
    )
    table_grad = jnp.einsum(
        "btjn,btjd->nd",
        basis_hot,
        basis_grad.reshape(basis_count, tile_count_n, TILE, feat_width),
        precision=three_pass,
        preferred_element_type=jnp.float32,
    )

    grad_heads = cotangent.reshape(node_rows, HEADS, HEAD_DIM)
    num_grad = grad_heads / normalizer[:, :, None]
    den_grad = -jnp.sum(grad_heads * attended, axis=2) / normalizer
    dkv_part = jnp.einsum("ihd,ihe->hde", exp_query, num_grad, precision=precise)
    dks_part = jnp.einsum("ihd,ih->hd", exp_query, den_grad, precision=precise)
    dks_size = dks_part.size
    reduced = lax.psum(
        jnp.concatenate([dkv_part.reshape(-1), dks_part.reshape(-1), coef_part.reshape(-1)]),
        ("outer", "nodes"),
    )
    dkv_sum = reduced[:kv_size].reshape(dkv_part.shape)
    dks_sum = reduced[kv_size : kv_size + dks_size].reshape(dks_part.shape)
    coef_sum = reduced[kv_size + dks_size :].reshape(coef_part.shape)
    query_side = (
        jnp.einsum("ihe,hde->ihd", num_grad, kv_sum, precision=precise)
        + den_grad[:, :, None] * ks_sum[None]
    )
    key_side = jnp.einsum("ihe,hde->ihd", values, dkv_sum, precision=precise) + dks_sum[None]
    value_side = jnp.einsum("ihd,hde->ihe", exp_key, dkv_sum, precision=precise)
    proj_grad = jnp.concatenate(
        [
            (query_side * exp_query).reshape(node_rows, feat_width),
            (key_side * exp_key).reshape(node_rows, feat_width),
            value_side.reshape(node_rows, feat_width),
        ],
        axis=1,
    ).astype(jnp.bfloat16)
    grad_x = jnp.einsum("mc,dc->md", proj_grad, w_all, preferred_element_type=jnp.float32)
    returned = lax.all_to_all(
        table_grad[node_rows:].reshape(peer_count, peer_slots, feat_width),
        "nodes",
        split_axis=0,
        concat_axis=0,
        tiled=True,
    )
    back_grad = jnp.einsum(
        "km,kd->md",
        pick.astype(jnp.float32),
        returned.reshape(-1, feat_width),
        precision=three_pass,
        preferred_element_type=jnp.float32,
    )
    grad_x = grad_x + table_grad[:node_rows] + back_grad
    feat_part = jnp.einsum("mc,me->ce", features, proj_grad, preferred_element_type=jnp.float32)
    basis_part = jnp.einsum("bmc,me->cbe", basis_in, cot_half, preferred_element_type=jnp.float32)
    stacked = lax.psum(
        jnp.concatenate([feat_part, basis_part.reshape(feat_width, -1)], axis=1), ("outer", "nodes")
    )
    stacked = stacked * norm_scale
    query_grad = stacked[:, :feat_width]
    key_grad = stacked[:, feat_width : 2 * feat_width]
    value_grad = stacked[:, 2 * feat_width : 3 * feat_width]
    bases_grad = jnp.transpose(
        stacked[:, 3 * feat_width :].reshape(feat_width, basis_count, feat_width), (1, 0, 2)
    )
    coef_grad = coef_sum * norm_scale
    return (layer_out, grad_x, query_grad, key_grad, value_grad, bases_grad, coef_grad)


def solution(mesh):
    in_specs = (
        P(("outer", "nodes"), None),
        P(),
        P(),
        P(),
        P(),
        P(),
        P(("outer", "nodes"), None, None),
        P(("outer", "nodes"), None, None, None),
        P(("outer", "nodes"), None, None, None),
        P(("outer", "nodes"), None, None),
        P(("outer", "nodes"), None),
    )
    out_specs = (P(("outer", "nodes"), None), P(("outer", "nodes"), None), P(), P(), P(), P(), P())
    return jax.shard_map(
        per_device, mesh=mesh, in_specs=in_specs, out_specs=out_specs, check_vma=False
    )
```

```python
import math

import jax
import jax.numpy as jnp
from jax import lax
from jax.sharding import PartitionSpec as P

HEADS = 8
HEAD_DIM = 64
TILE = 128


precise = lax.Precision.HIGHEST
three_pass = lax.Precision.HIGH


def group_sum(flat):
    axes = ("outer", "nodes")
    devices = lax.axis_size("outer") * lax.axis_size("nodes")
    size = flat.shape[0]
    chunk = -(-size // (devices * 128)) * 128
    padded = jnp.pad(flat, (0, devices * chunk - size)).reshape(devices, chunk)
    received = lax.all_to_all(padded, axes, split_axis=0, concat_axis=0, tiled=True)
    mine = jnp.sum(received, axis=0, keepdims=True)
    spread = jnp.broadcast_to(mine, (devices, chunk))
    gathered = lax.all_to_all(spread, axes, split_axis=0, concat_axis=0, tiled=True)
    return gathered.reshape(-1)[:size]


def per_device(
    features,
    w_query,
    w_key,
    w_value,
    bases,
    rel_coef,
    send_rows,
    tile_src,
    tile_dst,
    tile_count,
    cotangent,
):
    node_rows, feat_width = features.shape
    peer_count = lax.axis_size("nodes")
    total_nodes = node_rows * peer_count * lax.axis_size("outer")
    norm_scale = 1.0 / math.sqrt(total_nodes)
    basis_count = bases.shape[0]
    send_list = send_rows[0]
    peer_slots = send_list.shape[1]
    send_flat = send_list.reshape(-1)
    pick = (send_flat[:, None] == jnp.arange(node_rows)[None, :]).astype(jnp.bfloat16)
    outgoing = jnp.dot(pick, features, preferred_element_type=jnp.float32).astype(jnp.bfloat16)
    outgoing = outgoing.reshape(peer_count, peer_slots, feat_width)
    incoming = lax.all_to_all(outgoing, "nodes", split_axis=0, concat_axis=0, tiled=True)
    halo_table = jnp.concatenate([features, incoming.reshape(-1, feat_width)], axis=0)
    table_rows = halo_table.shape[0]

    w_all = jnp.concatenate([w_query, w_key, w_value], axis=1)
    projected = jnp.dot(features, w_all, preferred_element_type=jnp.float32)
    exp_query = jnp.exp(projected[:, :feat_width]).reshape(node_rows, HEADS, HEAD_DIM)
    exp_key = jnp.exp(projected[:, feat_width : 2 * feat_width]).reshape(node_rows, HEADS, HEAD_DIM)
    values = projected[:, 2 * feat_width :].reshape(node_rows, HEADS, HEAD_DIM)
    kv_part = jnp.einsum("ihd,ihe->hde", exp_key, values, precision=precise)
    ks_part = jnp.sum(exp_key, axis=0)
    kv_size = kv_part.size
    summary = group_sum(jnp.concatenate([kv_part.reshape(-1), ks_part.reshape(-1)]))
    kv_sum = summary[:kv_size].reshape(kv_part.shape)
    ks_sum = summary[kv_size:].reshape(ks_part.shape)

    src_all = tile_src[0]
    dst_all = tile_dst[0]
    count_all = tile_count[0]
    rel_count, tile_count_n, slot_count = src_all.shape
    live = jnp.arange(slot_count)[None, None, :] < count_all[:, :, None]
    dst_hot = (dst_all[..., None] == jnp.arange(TILE)).astype(jnp.bfloat16) * live[
        ..., None
    ].astype(jnp.bfloat16)
    src_hot = (src_all[..., None] == jnp.arange(table_rows)).astype(jnp.bfloat16)
    edge_counts = jnp.einsum(
        "rtej,rten->rtjn", dst_hot, src_hot, preferred_element_type=jnp.float32
    ).astype(jnp.bfloat16)
    degree = jnp.maximum(jnp.sum(dst_hot.astype(jnp.float32), axis=2), 1.0)
    row_sums = jnp.einsum(
        "rtjn,nd->rtjd", edge_counts, halo_table, preferred_element_type=jnp.float32
    )
    aggregate = (row_sums / degree[..., None]).reshape(rel_count, node_rows, feat_width)
    basis_in = jnp.einsum("rb,rmd->bmd", rel_coef, aggregate, precision=precise).astype(
        jnp.bfloat16
    )
    conv_out = jnp.einsum("bmd,bde->me", basis_in, bases, preferred_element_type=jnp.float32)
    normalizer = jnp.einsum("ihd,hd->ih", exp_query, ks_sum, precision=precise)
    attended = (
        jnp.einsum("ihd,hde->ihe", exp_query, kv_sum, precision=precise) / normalizer[:, :, None]
    )
    layer_out = attended.reshape(node_rows, feat_width) + conv_out
    cot_half = cotangent.astype(jnp.bfloat16)
    basis_grad = jnp.einsum("me,bde->bmd", cot_half, bases, preferred_element_type=jnp.float32)
    coef_part = jnp.sum(aggregate[:, None] * basis_grad[None], axis=(2, 3))
    weight_rb = rel_coef[:, :, None, None] / degree[:, None, :, :]
    basis_hot = jnp.stack(
        [
            jnp.sum(weight_rb[:, b, :, :, None] * edge_counts.astype(jnp.float32), axis=0)
            for b in range(basis_count)
        ]
    )
    table_grad = jnp.einsum(
        "btjn,btjd->nd",
        basis_hot,
        basis_grad.reshape(basis_count, tile_count_n, TILE, feat_width),
        precision=three_pass,
        preferred_element_type=jnp.float32,
    )

    grad_heads = cotangent.reshape(node_rows, HEADS, HEAD_DIM)
    num_grad = grad_heads / normalizer[:, :, None]
    den_grad = -jnp.sum(grad_heads * attended, axis=2) / normalizer
    dkv_part = jnp.einsum("ihd,ihe->hde", exp_query, num_grad, precision=precise)
    dks_part = jnp.einsum("ihd,ih->hd", exp_query, den_grad, precision=precise)
    dks_size = dks_part.size
    reduced = group_sum(
        jnp.concatenate([dkv_part.reshape(-1), dks_part.reshape(-1), coef_part.reshape(-1)])
    )
    dkv_sum = reduced[:kv_size].reshape(dkv_part.shape)
    dks_sum = reduced[kv_size : kv_size + dks_size].reshape(dks_part.shape)
    coef_sum = reduced[kv_size + dks_size :].reshape(coef_part.shape)
    query_side = (
        jnp.einsum("ihe,hde->ihd", num_grad, kv_sum, precision=precise)
        + den_grad[:, :, None] * ks_sum[None]
    )
    key_side = jnp.einsum("ihe,hde->ihd", values, dkv_sum, precision=precise) + dks_sum[None]
    value_side = jnp.einsum("ihd,hde->ihe", exp_key, dkv_sum, precision=precise)
    proj_grad = jnp.concatenate(
        [
            (query_side * exp_query).reshape(node_rows, feat_width),
            (key_side * exp_key).reshape(node_rows, feat_width),
            value_side.reshape(node_rows, feat_width),
        ],
        axis=1,
    ).astype(jnp.bfloat16)
    grad_x = jnp.einsum("mc,dc->md", proj_grad, w_all, preferred_element_type=jnp.float32)
    returned = lax.all_to_all(
        table_grad[node_rows:].reshape(peer_count, peer_slots, feat_width),
        "nodes",
        split_axis=0,
        concat_axis=0,
        tiled=True,
    )
    back_grad = jnp.einsum(
        "km,kd->md",
        pick.astype(jnp.float32),
        returned.reshape(-1, feat_width),
        precision=three_pass,
        preferred_element_type=jnp.float32,
    )
    grad_x = grad_x + table_grad[:node_rows] + back_grad
    feat_part = jnp.einsum("mc,me->ce", features, proj_grad, preferred_element_type=jnp.float32)
    basis_part = jnp.einsum("bmc,me->cbe", basis_in, cot_half, preferred_element_type=jnp.float32)
    stacked = group_sum(
        jnp.concatenate([feat_part, basis_part.reshape(feat_width, -1)], axis=1).reshape(-1)
    ).reshape(feat_width, -1)
    stacked = stacked * norm_scale
    query_grad = stacked[:, :feat_width]
    key_grad = stacked[:, feat_width : 2 * feat_width]
    value_grad = stacked[:, 2 * feat_width : 3 * feat_width]
    bases_grad = jnp.transpose(
        stacked[:, 3 * feat_width :].reshape(feat_width, basis_count, feat_width), (1, 0, 2)
    )
    coef_grad = coef_sum * norm_scale
    return (layer_out, grad_x, query_grad, key_grad, value_grad, bases_grad, coef_grad)


def solution(mesh):
    in_specs = (
        P(("outer", "nodes"), None),
        P(),
        P(),
        P(),
        P(),
        P(),
        P(("outer", "nodes"), None, None),
        P(("outer", "nodes"), None, None, None),
        P(("outer", "nodes"), None, None, None),
        P(("outer", "nodes"), None, None),
        P(("outer", "nodes"), None),
    )
    out_specs = (P(("outer", "nodes"), None), P(("outer", "nodes"), None), P(), P(), P(), P(), P())
    return jax.shard_map(
        per_device, mesh=mesh, in_specs=in_specs, out_specs=out_specs, check_vma=False
    )
```

```python
import math

import jax
import jax.numpy as jnp
from jax import lax
from jax.sharding import PartitionSpec as P

HEADS = 8
HEAD_DIM = 64
TILE = 128


precise = lax.Precision.HIGHEST
three_pass = lax.Precision.HIGH


def axis_sum(flat, axis):
    devices = lax.axis_size(axis)
    size = flat.shape[0]
    chunk = -(-size // (devices * 128)) * 128
    padded = jnp.pad(flat, (0, devices * chunk - size)).reshape(devices, chunk)
    received = lax.all_to_all(padded, axis, split_axis=0, concat_axis=0, tiled=True)
    mine = jnp.sum(received, axis=0, keepdims=True)
    return mine, chunk


def axis_gather(mine, axis, size):
    devices = lax.axis_size(axis)
    spread = jnp.broadcast_to(mine, (devices, mine.shape[1]))
    gathered = lax.all_to_all(spread, axis, split_axis=0, concat_axis=0, tiled=True)
    return gathered.reshape(-1)[:size]


def group_sum(flat):
    size = flat.shape[0]
    core_part, _ = axis_sum(flat, "outer")
    core_size = core_part.shape[1]
    chip_part, _ = axis_sum(core_part.reshape(-1), "nodes")
    core_total = axis_gather(chip_part, "nodes", core_size)
    return axis_gather(core_total[None], "outer", size)


def per_device(
    features,
    w_query,
    w_key,
    w_value,
    bases,
    rel_coef,
    send_rows,
    tile_src,
    tile_dst,
    tile_count,
    cotangent,
):
    node_rows, feat_width = features.shape
    peer_count = lax.axis_size("nodes")
    total_nodes = node_rows * peer_count * lax.axis_size("outer")
    norm_scale = 1.0 / math.sqrt(total_nodes)
    basis_count = bases.shape[0]
    send_list = send_rows[0]
    peer_slots = send_list.shape[1]
    send_flat = send_list.reshape(-1)
    pick = (send_flat[:, None] == jnp.arange(node_rows)[None, :]).astype(jnp.bfloat16)
    outgoing = jnp.dot(pick, features, preferred_element_type=jnp.float32).astype(jnp.bfloat16)
    outgoing = outgoing.reshape(peer_count, peer_slots, feat_width)
    incoming = lax.all_to_all(outgoing, "nodes", split_axis=0, concat_axis=0, tiled=True)
    halo_table = jnp.concatenate([features, incoming.reshape(-1, feat_width)], axis=0)
    table_rows = halo_table.shape[0]

    w_all = jnp.concatenate([w_query, w_key, w_value], axis=1)
    projected = jnp.dot(features, w_all, preferred_element_type=jnp.float32)
    exp_query = jnp.exp(projected[:, :feat_width]).reshape(node_rows, HEADS, HEAD_DIM)
    exp_key = jnp.exp(projected[:, feat_width : 2 * feat_width]).reshape(node_rows, HEADS, HEAD_DIM)
    values = projected[:, 2 * feat_width :].reshape(node_rows, HEADS, HEAD_DIM)
    kv_part = jnp.einsum("ihd,ihe->hde", exp_key, values, precision=precise)
    ks_part = jnp.sum(exp_key, axis=0)
    kv_size = kv_part.size
    summary = group_sum(jnp.concatenate([kv_part.reshape(-1), ks_part.reshape(-1)]))
    kv_sum = summary[:kv_size].reshape(kv_part.shape)
    ks_sum = summary[kv_size:].reshape(ks_part.shape)

    src_all = tile_src[0]
    dst_all = tile_dst[0]
    count_all = tile_count[0]
    rel_count, tile_count_n, slot_count = src_all.shape
    live = jnp.arange(slot_count)[None, None, :] < count_all[:, :, None]
    dst_hot = (dst_all[..., None] == jnp.arange(TILE)).astype(jnp.bfloat16) * live[
        ..., None
    ].astype(jnp.bfloat16)
    src_hot = (src_all[..., None] == jnp.arange(table_rows)).astype(jnp.bfloat16)
    edge_counts = jnp.einsum(
        "rtej,rten->rtjn", dst_hot, src_hot, preferred_element_type=jnp.float32
    ).astype(jnp.bfloat16)
    degree = jnp.maximum(jnp.sum(dst_hot.astype(jnp.float32), axis=2), 1.0)
    row_sums = jnp.einsum(
        "rtjn,nd->rtjd", edge_counts, halo_table, preferred_element_type=jnp.float32
    )
    aggregate = (row_sums / degree[..., None]).reshape(rel_count, node_rows, feat_width)
    basis_in = jnp.einsum("rb,rmd->bmd", rel_coef, aggregate, precision=precise).astype(
        jnp.bfloat16
    )
    conv_out = jnp.einsum("bmd,bde->me", basis_in, bases, preferred_element_type=jnp.float32)
    normalizer = jnp.einsum("ihd,hd->ih", exp_query, ks_sum, precision=precise)
    attended = (
        jnp.einsum("ihd,hde->ihe", exp_query, kv_sum, precision=precise) / normalizer[:, :, None]
    )
    layer_out = attended.reshape(node_rows, feat_width) + conv_out
    cot_half = cotangent.astype(jnp.bfloat16)
    basis_grad = jnp.einsum("me,bde->bmd", cot_half, bases, preferred_element_type=jnp.float32)
    coef_part = jnp.sum(aggregate[:, None] * basis_grad[None], axis=(2, 3))
    weight_rb = rel_coef[:, :, None, None] / degree[:, None, :, :]
    basis_hot = jnp.stack(
        [
            jnp.sum(weight_rb[:, b, :, :, None] * edge_counts.astype(jnp.float32), axis=0)
            for b in range(basis_count)
        ]
    )
    table_grad = jnp.einsum(
        "btjn,btjd->nd",
        basis_hot,
        basis_grad.reshape(basis_count, tile_count_n, TILE, feat_width),
        precision=three_pass,
        preferred_element_type=jnp.float32,
    )

    grad_heads = cotangent.reshape(node_rows, HEADS, HEAD_DIM)
    num_grad = grad_heads / normalizer[:, :, None]
    den_grad = -jnp.sum(grad_heads * attended, axis=2) / normalizer
    dkv_part = jnp.einsum("ihd,ihe->hde", exp_query, num_grad, precision=precise)
    dks_part = jnp.einsum("ihd,ih->hd", exp_query, den_grad, precision=precise)
    dks_size = dks_part.size
    reduced = group_sum(
        jnp.concatenate([dkv_part.reshape(-1), dks_part.reshape(-1), coef_part.reshape(-1)])
    )
    dkv_sum = reduced[:kv_size].reshape(dkv_part.shape)
    dks_sum = reduced[kv_size : kv_size + dks_size].reshape(dks_part.shape)
    coef_sum = reduced[kv_size + dks_size :].reshape(coef_part.shape)
    query_side = (
        jnp.einsum("ihe,hde->ihd", num_grad, kv_sum, precision=precise)
        + den_grad[:, :, None] * ks_sum[None]
    )
    key_side = jnp.einsum("ihe,hde->ihd", values, dkv_sum, precision=precise) + dks_sum[None]
    value_side = jnp.einsum("ihd,hde->ihe", exp_key, dkv_sum, precision=precise)
    proj_grad = jnp.concatenate(
        [
            (query_side * exp_query).reshape(node_rows, feat_width),
            (key_side * exp_key).reshape(node_rows, feat_width),
            value_side.reshape(node_rows, feat_width),
        ],
        axis=1,
    ).astype(jnp.bfloat16)
    grad_x = jnp.einsum("mc,dc->md", proj_grad, w_all, preferred_element_type=jnp.float32)
    returned = lax.all_to_all(
        table_grad[node_rows:].reshape(peer_count, peer_slots, feat_width),
        "nodes",
        split_axis=0,
        concat_axis=0,
        tiled=True,
    )
    back_grad = jnp.einsum(
        "km,kd->md",
        pick.astype(jnp.float32),
        returned.reshape(-1, feat_width),
        precision=three_pass,
        preferred_element_type=jnp.float32,
    )
    grad_x = grad_x + table_grad[:node_rows] + back_grad
    basis_part = jnp.einsum("bmc,me->cbe", basis_in, cot_half, preferred_element_type=jnp.float32)
    query_block = proj_grad[:, :feat_width]
    query_part = jnp.einsum("mc,me->ce", features, query_block, preferred_element_type=jnp.float32)
    early = group_sum(
        jnp.concatenate([query_part, basis_part.reshape(feat_width, -1)], axis=1).reshape(-1)
    ).reshape(feat_width, -1)
    late_part = jnp.einsum(
        "mc,me->ce", features, proj_grad[:, feat_width:], preferred_element_type=jnp.float32
    )
    late = group_sum(late_part.reshape(-1)).reshape(feat_width, -1)
    early = early * norm_scale
    late = late * norm_scale
    query_grad = early[:, :feat_width]
    key_grad = late[:, :feat_width]
    value_grad = late[:, feat_width:]
    bases_grad = jnp.transpose(
        early[:, feat_width:].reshape(feat_width, basis_count, feat_width), (1, 0, 2)
    )
    coef_grad = coef_sum * norm_scale
    return (layer_out, grad_x, query_grad, key_grad, value_grad, bases_grad, coef_grad)


def solution(mesh):
    in_specs = (
        P(("outer", "nodes"), None),
        P(),
        P(),
        P(),
        P(),
        P(),
        P(("outer", "nodes"), None, None),
        P(("outer", "nodes"), None, None, None),
        P(("outer", "nodes"), None, None, None),
        P(("outer", "nodes"), None, None),
        P(("outer", "nodes"), None),
    )
    out_specs = (P(("outer", "nodes"), None), P(("outer", "nodes"), None), P(), P(), P(), P(), P())
    return jax.shard_map(
        per_device, mesh=mesh, in_specs=in_specs, out_specs=out_specs, check_vma=False
    )
```

```python
import math

import jax
import jax.numpy as jnp
from jax import lax
from jax.sharding import PartitionSpec as P

HEADS = 8
HEAD_DIM = 64
TILE = 128


precise = lax.Precision.HIGHEST
three_pass = lax.Precision.HIGH


def group_sum(flat, wire=jnp.float32):
    axes = ("outer", "nodes")
    devices = lax.axis_size("outer") * lax.axis_size("nodes")
    size = flat.shape[0]
    chunk = -(-size // (devices * 128)) * 128
    padded = jnp.pad(flat, (0, devices * chunk - size)).reshape(devices, chunk)
    received = lax.all_to_all(padded.astype(wire), axes, split_axis=0, concat_axis=0, tiled=True)
    mine = jnp.sum(received.astype(jnp.float32), axis=0, keepdims=True)
    spread = jnp.broadcast_to(mine.astype(wire), (devices, chunk))
    gathered = lax.all_to_all(spread, axes, split_axis=0, concat_axis=0, tiled=True)
    return gathered.reshape(-1)[:size].astype(jnp.float32)


def per_device(
    features,
    w_query,
    w_key,
    w_value,
    bases,
    rel_coef,
    send_rows,
    tile_src,
    tile_dst,
    tile_count,
    cotangent,
):
    node_rows, feat_width = features.shape
    peer_count = lax.axis_size("nodes")
    total_nodes = node_rows * peer_count * lax.axis_size("outer")
    norm_scale = 1.0 / math.sqrt(total_nodes)
    basis_count = bases.shape[0]
    send_list = send_rows[0]
    peer_slots = send_list.shape[1]
    send_flat = send_list.reshape(-1)
    pick = (send_flat[:, None] == jnp.arange(node_rows)[None, :]).astype(jnp.bfloat16)
    outgoing = jnp.dot(pick, features, preferred_element_type=jnp.float32).astype(jnp.bfloat16)
    outgoing = outgoing.reshape(peer_count, peer_slots, feat_width)
    incoming = lax.all_to_all(outgoing, "nodes", split_axis=0, concat_axis=0, tiled=True)
    halo_table = jnp.concatenate([features, incoming.reshape(-1, feat_width)], axis=0)
    table_rows = halo_table.shape[0]

    w_all = jnp.concatenate([w_query, w_key, w_value], axis=1)
    projected = jnp.dot(features, w_all, preferred_element_type=jnp.float32)
    exp_query = jnp.exp(projected[:, :feat_width]).reshape(node_rows, HEADS, HEAD_DIM)
    exp_key = jnp.exp(projected[:, feat_width : 2 * feat_width]).reshape(node_rows, HEADS, HEAD_DIM)
    values = projected[:, 2 * feat_width :].reshape(node_rows, HEADS, HEAD_DIM)
    kv_part = jnp.einsum("ihd,ihe->hde", exp_key, values, precision=precise)
    ks_part = jnp.sum(exp_key, axis=0)
    kv_size = kv_part.size
    summary = group_sum(jnp.concatenate([kv_part.reshape(-1), ks_part.reshape(-1)]))
    kv_sum = summary[:kv_size].reshape(kv_part.shape)
    ks_sum = summary[kv_size:].reshape(ks_part.shape)

    src_all = tile_src[0]
    dst_all = tile_dst[0]
    count_all = tile_count[0]
    rel_count, tile_count_n, slot_count = src_all.shape
    live = jnp.arange(slot_count)[None, None, :] < count_all[:, :, None]
    dst_hot = (dst_all[..., None] == jnp.arange(TILE)).astype(jnp.bfloat16) * live[
        ..., None
    ].astype(jnp.bfloat16)
    src_hot = (src_all[..., None] == jnp.arange(table_rows)).astype(jnp.bfloat16)
    edge_counts = jnp.einsum(
        "rtej,rten->rtjn", dst_hot, src_hot, preferred_element_type=jnp.float32
    ).astype(jnp.bfloat16)
    degree = jnp.maximum(jnp.sum(dst_hot.astype(jnp.float32), axis=2), 1.0)
    row_sums = jnp.einsum(
        "rtjn,nd->rtjd", edge_counts, halo_table, preferred_element_type=jnp.float32
    )
    aggregate = (row_sums / degree[..., None]).reshape(rel_count, node_rows, feat_width)
    basis_in = jnp.einsum("rb,rmd->bmd", rel_coef, aggregate, precision=precise).astype(
        jnp.bfloat16
    )
    conv_out = jnp.einsum("bmd,bde->me", basis_in, bases, preferred_element_type=jnp.float32)
    normalizer = jnp.einsum("ihd,hd->ih", exp_query, ks_sum, precision=precise)
    attended = (
        jnp.einsum("ihd,hde->ihe", exp_query, kv_sum, precision=precise) / normalizer[:, :, None]
    )
    layer_out = attended.reshape(node_rows, feat_width) + conv_out
    cot_half = cotangent.astype(jnp.bfloat16)
    basis_grad = jnp.einsum("me,bde->bmd", cot_half, bases, preferred_element_type=jnp.float32)
    coef_part = jnp.sum(aggregate[:, None] * basis_grad[None], axis=(2, 3))
    weight_rb = rel_coef[:, :, None, None] / degree[:, None, :, :]
    basis_hot = jnp.stack(
        [
            jnp.sum(weight_rb[:, b, :, :, None] * edge_counts.astype(jnp.float32), axis=0)
            for b in range(basis_count)
        ]
    )
    table_grad = jnp.einsum(
        "btjn,btjd->nd",
        basis_hot,
        basis_grad.reshape(basis_count, tile_count_n, TILE, feat_width),
        precision=three_pass,
        preferred_element_type=jnp.float32,
    )

    grad_heads = cotangent.reshape(node_rows, HEADS, HEAD_DIM)
    num_grad = grad_heads / normalizer[:, :, None]
    den_grad = -jnp.sum(grad_heads * attended, axis=2) / normalizer
    dkv_part = jnp.einsum("ihd,ihe->hde", exp_query, num_grad, precision=precise)
    dks_part = jnp.einsum("ihd,ih->hd", exp_query, den_grad, precision=precise)
    dks_size = dks_part.size
    reduced = group_sum(
        jnp.concatenate([dkv_part.reshape(-1), dks_part.reshape(-1), coef_part.reshape(-1)])
    )
    dkv_sum = reduced[:kv_size].reshape(dkv_part.shape)
    dks_sum = reduced[kv_size : kv_size + dks_size].reshape(dks_part.shape)
    coef_sum = reduced[kv_size + dks_size :].reshape(coef_part.shape)
    query_side = (
        jnp.einsum("ihe,hde->ihd", num_grad, kv_sum, precision=precise)
        + den_grad[:, :, None] * ks_sum[None]
    )
    key_side = jnp.einsum("ihe,hde->ihd", values, dkv_sum, precision=precise) + dks_sum[None]
    value_side = jnp.einsum("ihd,hde->ihe", exp_key, dkv_sum, precision=precise)
    proj_grad = jnp.concatenate(
        [
            (query_side * exp_query).reshape(node_rows, feat_width),
            (key_side * exp_key).reshape(node_rows, feat_width),
            value_side.reshape(node_rows, feat_width),
        ],
        axis=1,
    ).astype(jnp.bfloat16)
    grad_x = jnp.einsum("mc,dc->md", proj_grad, w_all, preferred_element_type=jnp.float32)
    returned = lax.all_to_all(
        table_grad[node_rows:].astype(jnp.bfloat16).reshape(peer_count, peer_slots, feat_width),
        "nodes",
        split_axis=0,
        concat_axis=0,
        tiled=True,
    )
    back_grad = jnp.einsum(
        "km,kd->md", pick, returned.reshape(-1, feat_width), preferred_element_type=jnp.float32
    )
    grad_x = grad_x + table_grad[:node_rows] + back_grad
    feat_part = jnp.einsum("mc,me->ce", features, proj_grad, preferred_element_type=jnp.float32)
    basis_part = jnp.einsum("bmc,me->cbe", basis_in, cot_half, preferred_element_type=jnp.float32)
    stacked = group_sum(
        jnp.concatenate([feat_part, basis_part.reshape(feat_width, -1)], axis=1).reshape(-1),
        jnp.bfloat16,
    ).reshape(feat_width, -1)
    stacked = stacked * norm_scale
    query_grad = stacked[:, :feat_width]
    key_grad = stacked[:, feat_width : 2 * feat_width]
    value_grad = stacked[:, 2 * feat_width : 3 * feat_width]
    bases_grad = jnp.transpose(
        stacked[:, 3 * feat_width :].reshape(feat_width, basis_count, feat_width), (1, 0, 2)
    )
    coef_grad = coef_sum * norm_scale
    return (layer_out, grad_x, query_grad, key_grad, value_grad, bases_grad, coef_grad)


def solution(mesh):
    in_specs = (
        P(("outer", "nodes"), None),
        P(),
        P(),
        P(),
        P(),
        P(),
        P(("outer", "nodes"), None, None),
        P(("outer", "nodes"), None, None, None),
        P(("outer", "nodes"), None, None, None),
        P(("outer", "nodes"), None, None),
        P(("outer", "nodes"), None),
    )
    out_specs = (P(("outer", "nodes"), None), P(("outer", "nodes"), None), P(), P(), P(), P(), P())
    return jax.shard_map(
        per_device, mesh=mesh, in_specs=in_specs, out_specs=out_specs, check_vma=False
    )
```

```python
import math

import jax
import jax.numpy as jnp
from jax import lax
from jax.sharding import PartitionSpec as P

HEADS = 8
HEAD_DIM = 64
TILE = 128


precise = lax.Precision.HIGHEST
three_pass = lax.Precision.HIGH


def group_sum(flat):
    axes = ("outer", "nodes")
    devices = lax.axis_size("outer") * lax.axis_size("nodes")
    size = flat.shape[0]
    chunk = -(-size // (devices * 128)) * 128
    padded = jnp.pad(flat, (0, devices * chunk - size)).reshape(devices, chunk)
    received = lax.all_to_all(padded, axes, split_axis=0, concat_axis=0, tiled=True)
    mine = jnp.sum(received, axis=0, keepdims=True)
    spread = jnp.broadcast_to(mine, (devices, chunk))
    gathered = lax.all_to_all(spread, axes, split_axis=0, concat_axis=0, tiled=True)
    return gathered.reshape(-1)[:size]


def block_sum(block):
    axes = ("outer", "nodes")
    devices = lax.axis_size("outer") * lax.axis_size("nodes")
    rows, cols = block.shape
    parts = devices // (rows // 8)
    width = cols // parts
    tiles = block.reshape(rows // 8, 8, parts, width).transpose(0, 2, 1, 3)
    tiles = tiles.reshape(devices, 8, width)
    received = lax.all_to_all(tiles, axes, split_axis=0, concat_axis=0, tiled=True)
    mine = jnp.sum(received, axis=0, keepdims=True)
    spread = jnp.broadcast_to(mine, (devices, 8, width))
    gathered = lax.all_to_all(spread, axes, split_axis=0, concat_axis=0, tiled=True)
    gathered = gathered.reshape(rows // 8, parts, 8, width).transpose(0, 2, 1, 3)
    return gathered.reshape(rows, cols)


def per_device(
    features,
    w_query,
    w_key,
    w_value,
    bases,
    rel_coef,
    send_rows,
    tile_src,
    tile_dst,
    tile_count,
    cotangent,
):
    node_rows, feat_width = features.shape
    peer_count = lax.axis_size("nodes")
    total_nodes = node_rows * peer_count * lax.axis_size("outer")
    norm_scale = 1.0 / math.sqrt(total_nodes)
    basis_count = bases.shape[0]
    send_list = send_rows[0]
    peer_slots = send_list.shape[1]
    send_flat = send_list.reshape(-1)
    pick = (send_flat[:, None] == jnp.arange(node_rows)[None, :]).astype(jnp.bfloat16)
    outgoing = jnp.dot(pick, features, preferred_element_type=jnp.float32).astype(jnp.bfloat16)
    outgoing = outgoing.reshape(peer_count, peer_slots, feat_width)
    incoming = lax.all_to_all(outgoing, "nodes", split_axis=0, concat_axis=0, tiled=True)
    halo_table = jnp.concatenate([features, incoming.reshape(-1, feat_width)], axis=0)
    table_rows = halo_table.shape[0]

    w_all = jnp.concatenate([w_query, w_key, w_value], axis=1)
    projected = jnp.dot(features, w_all, preferred_element_type=jnp.float32)
    exp_query = jnp.exp(projected[:, :feat_width]).reshape(node_rows, HEADS, HEAD_DIM)
    exp_key = jnp.exp(projected[:, feat_width : 2 * feat_width]).reshape(node_rows, HEADS, HEAD_DIM)
    values = projected[:, 2 * feat_width :].reshape(node_rows, HEADS, HEAD_DIM)
    kv_part = jnp.einsum("ihd,ihe->hde", exp_key, values, precision=precise)
    ks_part = jnp.sum(exp_key, axis=0)
    kv_size = kv_part.size
    summary = group_sum(jnp.concatenate([kv_part.reshape(-1), ks_part.reshape(-1)]))
    kv_sum = summary[:kv_size].reshape(kv_part.shape)
    ks_sum = summary[kv_size:].reshape(ks_part.shape)

    src_all = tile_src[0]
    dst_all = tile_dst[0]
    count_all = tile_count[0]
    rel_count, tile_count_n, slot_count = src_all.shape
    live = jnp.arange(slot_count)[None, None, :] < count_all[:, :, None]
    dst_hot = (dst_all[..., None] == jnp.arange(TILE)).astype(jnp.bfloat16) * live[
        ..., None
    ].astype(jnp.bfloat16)
    src_hot = (src_all[..., None] == jnp.arange(table_rows)).astype(jnp.bfloat16)
    edge_counts = jnp.einsum(
        "rtej,rten->rtjn", dst_hot, src_hot, preferred_element_type=jnp.float32
    ).astype(jnp.bfloat16)
    degree = jnp.maximum(jnp.sum(dst_hot.astype(jnp.float32), axis=2), 1.0)
    row_sums = jnp.einsum(
        "rtjn,nd->rtjd", edge_counts, halo_table, preferred_element_type=jnp.float32
    )
    aggregate = (row_sums / degree[..., None]).reshape(rel_count, node_rows, feat_width)
    basis_in = jnp.einsum("rb,rmd->bmd", rel_coef, aggregate, precision=precise).astype(
        jnp.bfloat16
    )
    conv_out = jnp.einsum("bmd,bde->me", basis_in, bases, preferred_element_type=jnp.float32)
    normalizer = jnp.einsum("ihd,hd->ih", exp_query, ks_sum, precision=precise)
    attended = (
        jnp.einsum("ihd,hde->ihe", exp_query, kv_sum, precision=precise) / normalizer[:, :, None]
    )
    layer_out = attended.reshape(node_rows, feat_width) + conv_out
    cot_half = cotangent.astype(jnp.bfloat16)
    basis_grad = jnp.einsum("me,bde->bmd", cot_half, bases, preferred_element_type=jnp.float32)
    coef_part = jnp.sum(aggregate[:, None] * basis_grad[None], axis=(2, 3))
    weight_rb = rel_coef[:, :, None, None] / degree[:, None, :, :]
    basis_hot = jnp.stack(
        [
            jnp.sum(weight_rb[:, b, :, :, None] * edge_counts.astype(jnp.float32), axis=0)
            for b in range(basis_count)
        ]
    )
    table_grad = jnp.einsum(
        "btjn,btjd->nd",
        basis_hot,
        basis_grad.reshape(basis_count, tile_count_n, TILE, feat_width),
        precision=three_pass,
        preferred_element_type=jnp.float32,
    )

    grad_heads = cotangent.reshape(node_rows, HEADS, HEAD_DIM)
    num_grad = grad_heads / normalizer[:, :, None]
    den_grad = -jnp.sum(grad_heads * attended, axis=2) / normalizer
    dkv_part = jnp.einsum("ihd,ihe->hde", exp_query, num_grad, precision=precise)
    dks_part = jnp.einsum("ihd,ih->hd", exp_query, den_grad, precision=precise)
    dks_size = dks_part.size
    reduced = group_sum(
        jnp.concatenate([dkv_part.reshape(-1), dks_part.reshape(-1), coef_part.reshape(-1)])
    )
    dkv_sum = reduced[:kv_size].reshape(dkv_part.shape)
    dks_sum = reduced[kv_size : kv_size + dks_size].reshape(dks_part.shape)
    coef_sum = reduced[kv_size + dks_size :].reshape(coef_part.shape)
    query_side = (
        jnp.einsum("ihe,hde->ihd", num_grad, kv_sum, precision=precise)
        + den_grad[:, :, None] * ks_sum[None]
    )
    key_side = jnp.einsum("ihe,hde->ihd", values, dkv_sum, precision=precise) + dks_sum[None]
    value_side = jnp.einsum("ihd,hde->ihe", exp_key, dkv_sum, precision=precise)
    proj_grad = jnp.concatenate(
        [
            (query_side * exp_query).reshape(node_rows, feat_width),
            (key_side * exp_key).reshape(node_rows, feat_width),
            value_side.reshape(node_rows, feat_width),
        ],
        axis=1,
    ).astype(jnp.bfloat16)
    grad_x = jnp.einsum("mc,dc->md", proj_grad, w_all, preferred_element_type=jnp.float32)
    returned = lax.all_to_all(
        table_grad[node_rows:].astype(jnp.bfloat16).reshape(peer_count, peer_slots, feat_width),
        "nodes",
        split_axis=0,
        concat_axis=0,
        tiled=True,
    )
    back_grad = jnp.einsum(
        "km,kd->md", pick, returned.reshape(-1, feat_width), preferred_element_type=jnp.float32
    )
    grad_x = grad_x + table_grad[:node_rows] + back_grad
    feat_part = jnp.einsum("mc,me->ce", features, proj_grad, preferred_element_type=jnp.float32)
    basis_part = jnp.einsum("bmc,me->cbe", basis_in, cot_half, preferred_element_type=jnp.float32)
    stacked = block_sum(jnp.concatenate([feat_part, basis_part.reshape(feat_width, -1)], axis=1))
    stacked = stacked * norm_scale
    query_grad = stacked[:, :feat_width]
    key_grad = stacked[:, feat_width : 2 * feat_width]
    value_grad = stacked[:, 2 * feat_width : 3 * feat_width]
    bases_grad = jnp.transpose(
        stacked[:, 3 * feat_width :].reshape(feat_width, basis_count, feat_width), (1, 0, 2)
    )
    coef_grad = coef_sum * norm_scale
    return (layer_out, grad_x, query_grad, key_grad, value_grad, bases_grad, coef_grad)


def solution(mesh):
    in_specs = (
        P(("outer", "nodes"), None),
        P(),
        P(),
        P(),
        P(),
        P(),
        P(("outer", "nodes"), None, None),
        P(("outer", "nodes"), None, None, None),
        P(("outer", "nodes"), None, None, None),
        P(("outer", "nodes"), None, None),
        P(("outer", "nodes"), None),
    )
    out_specs = (P(("outer", "nodes"), None), P(("outer", "nodes"), None), P(), P(), P(), P(), P())
    return jax.shard_map(
        per_device, mesh=mesh, in_specs=in_specs, out_specs=out_specs, check_vma=False
    )
```

```python
import math

import jax
import jax.numpy as jnp
from jax import lax
from jax.experimental import pallas as pl
from jax.experimental.pallas import tpu as pltpu
from jax.sharding import PartitionSpec as P

HEADS = 8
HEAD_DIM = 64
TILE = 128


precise = lax.Precision.HIGHEST
three_pass = lax.Precision.HIGH
NT = (((1,), (1,)), ((), ()))


def group_sum(flat):
    axes = ("outer", "nodes")
    devices = lax.axis_size("outer") * lax.axis_size("nodes")
    size = flat.shape[0]
    chunk = -(-size // (devices * 128)) * 128
    padded = jnp.pad(flat, (0, devices * chunk - size)).reshape(devices, chunk)
    received = lax.all_to_all(padded, axes, split_axis=0, concat_axis=0, tiled=True)
    mine = jnp.sum(received, axis=0, keepdims=True)
    spread = jnp.broadcast_to(mine, (devices, chunk))
    gathered = lax.all_to_all(spread, axes, split_axis=0, concat_axis=0, tiled=True)
    return gathered.reshape(-1)[:size]


def block_sum(block):
    axes = ("outer", "nodes")
    devices = lax.axis_size("outer") * lax.axis_size("nodes")
    rows, cols = block.shape
    parts = devices // (rows // 8)
    width = cols // parts
    tiles = block.reshape(rows // 8, 8, parts, width).transpose(0, 2, 1, 3)
    tiles = tiles.reshape(devices, 8, width)
    received = lax.all_to_all(tiles, axes, split_axis=0, concat_axis=0, tiled=True)
    mine = jnp.sum(received, axis=0, keepdims=True)
    spread = jnp.broadcast_to(mine, (devices, 8, width))
    gathered = lax.all_to_all(spread, axes, split_axis=0, concat_axis=0, tiled=True)
    gathered = gathered.reshape(rows // 8, parts, 8, width).transpose(0, 2, 1, 3)
    return gathered.reshape(rows, cols)


def split_dot(a, b):
    a_hi = a.astype(jnp.bfloat16)
    a_lo = (a - a_hi.astype(jnp.float32)).astype(jnp.bfloat16)
    b_hi = b.astype(jnp.bfloat16)
    b_lo = (b - b_hi.astype(jnp.float32)).astype(jnp.bfloat16)
    out = jnp.dot(a_hi, b_hi, preferred_element_type=jnp.float32)
    out += jnp.dot(a_hi, b_lo, preferred_element_type=jnp.float32)
    out += jnp.dot(a_lo, b_hi, preferred_element_type=jnp.float32)
    return out


def graph_kernel(coef_ref, src_ref, dst_ref, cnt_ref, table_ref, grad_ref, agg_ref, tgrad_ref, wsum_ref):
    tile = pl.program_id(0)
    rel_count = src_ref.shape[0]
    table_rows = table_ref.shape[0]
    basis_count = grad_ref.shape[0]

    @pl.when(tile == 0)
    def _():
        tgrad_ref[...] = jnp.zeros_like(tgrad_ref)

    wsum_ref[...] = jnp.zeros_like(wsum_ref)
    row_iota = lax.broadcasted_iota(jnp.int32, (table_rows, TILE), 0)
    node_iota = lax.broadcasted_iota(jnp.int32, (TILE, TILE), 0)
    slot_iota = lax.broadcasted_iota(jnp.int32, (TILE, TILE), 1)
    ones = jnp.ones((8, TILE), jnp.bfloat16)
    for r in range(rel_count):
        src_row = src_ref[r, 0]
        dst_row = dst_ref[r, 0]
        live = slot_iota < cnt_ref[r, tile]
        dst_t = ((node_iota == dst_row) & live).astype(jnp.bfloat16)
        src_t = (row_iota == src_row).astype(jnp.bfloat16)
        counts = lax.dot_general(dst_t, src_t, NT, preferred_element_type=jnp.float32)
        counts_t = lax.dot_general(src_t, dst_t, NT, preferred_element_type=jnp.float32)
        deg_col = jnp.maximum(jnp.sum(dst_t.astype(jnp.float32), axis=1, keepdims=True), 1.0)
        deg_row = jnp.maximum(
            lax.dot_general(ones, dst_t, NT, preferred_element_type=jnp.float32)[0:1], 1.0
        )
        sums = jnp.dot(counts.astype(jnp.bfloat16), table_ref[...], preferred_element_type=jnp.float32)
        agg_ref[r, 0] = sums / deg_col
        for b in range(basis_count):
            wsum_ref[b] += counts_t * (coef_ref[r, b] / deg_row)
    total = tgrad_ref[...]
    for b in range(basis_count):
        total += split_dot(wsum_ref[b], grad_ref[b])
    tgrad_ref[...] = total


def graph_conv(rel_coef, src, dst, cnt, table, basis_grad):
    rel_count, tiles, slots = src.shape
    table_rows, width = table.shape
    basis_count = basis_grad.shape[0]
    src4 = src.reshape(rel_count, tiles, 1, slots)
    dst4 = dst.reshape(rel_count, tiles, 1, slots)
    return pl.pallas_call(
        graph_kernel,
        grid=(tiles,),
        in_specs=[
            pl.BlockSpec(memory_space=pltpu.SMEM),
            pl.BlockSpec((rel_count, 1, 1, slots), lambda t: (0, t, 0, 0)),
            pl.BlockSpec((rel_count, 1, 1, slots), lambda t: (0, t, 0, 0)),
            pl.BlockSpec(memory_space=pltpu.SMEM),
            pl.BlockSpec((table_rows, width), lambda t: (0, 0)),
            pl.BlockSpec((basis_count, TILE, width), lambda t: (0, t, 0)),
        ],
        out_specs=[
            pl.BlockSpec((rel_count, 1, TILE, width), lambda t: (0, t, 0, 0)),
            pl.BlockSpec((table_rows, width), lambda t: (0, 0)),
        ],
        out_shape=[
            jax.ShapeDtypeStruct((rel_count, tiles, TILE, width), jnp.float32),
            jax.ShapeDtypeStruct((table_rows, width), jnp.float32),
        ],
        scratch_shapes=[pltpu.VMEM((basis_count, table_rows, TILE), jnp.float32)],
        compiler_params=pltpu.CompilerParams(
            dimension_semantics=("arbitrary",), vmem_limit_bytes=60 * 1024 * 1024
        ),
    )(rel_coef, src4, dst4, cnt, table, basis_grad)


def per_device(
    features,
    w_query,
    w_key,
    w_value,
    bases,
    rel_coef,
    send_rows,
    tile_src,
    tile_dst,
    tile_count,
    cotangent,
):
    node_rows, feat_width = features.shape
    peer_count = lax.axis_size("nodes")
    total_nodes = node_rows * peer_count * lax.axis_size("outer")
    norm_scale = 1.0 / math.sqrt(total_nodes)
    basis_count = bases.shape[0]
    send_list = send_rows[0]
    peer_slots = send_list.shape[1]
    send_flat = send_list.reshape(-1)
    pick = (send_flat[:, None] == jnp.arange(node_rows)[None, :]).astype(jnp.bfloat16)
    outgoing = jnp.dot(pick, features, preferred_element_type=jnp.float32).astype(jnp.bfloat16)
    outgoing = outgoing.reshape(peer_count, peer_slots, feat_width)
    incoming = lax.all_to_all(outgoing, "nodes", split_axis=0, concat_axis=0, tiled=True)
    halo_table = jnp.concatenate([features, incoming.reshape(-1, feat_width)], axis=0)
    table_rows = halo_table.shape[0]

    w_all = jnp.concatenate([w_query, w_key, w_value], axis=1)
    projected = jnp.dot(features, w_all, preferred_element_type=jnp.float32)
    exp_query = jnp.exp(projected[:, :feat_width]).reshape(node_rows, HEADS, HEAD_DIM)
    exp_key = jnp.exp(projected[:, feat_width : 2 * feat_width]).reshape(node_rows, HEADS, HEAD_DIM)
    values = projected[:, 2 * feat_width :].reshape(node_rows, HEADS, HEAD_DIM)
    kv_part = jnp.einsum("ihd,ihe->hde", exp_key, values, precision=precise)
    ks_part = jnp.sum(exp_key, axis=0)
    kv_size = kv_part.size
    summary = group_sum(jnp.concatenate([kv_part.reshape(-1), ks_part.reshape(-1)]))
    kv_sum = summary[:kv_size].reshape(kv_part.shape)
    ks_sum = summary[kv_size:].reshape(ks_part.shape)

    cot_half = cotangent.astype(jnp.bfloat16)
    basis_grad = jnp.einsum("me,bde->bmd", cot_half, bases, preferred_element_type=jnp.float32)
    rel_count = tile_src.shape[1]
    aggregate, table_grad = graph_conv(
        rel_coef, tile_src[0], tile_dst[0], tile_count[0], halo_table, basis_grad
    )
    aggregate = aggregate.reshape(rel_count, node_rows, feat_width)
    basis_in = jnp.einsum("rb,rmd->bmd", rel_coef, aggregate, precision=precise).astype(
        jnp.bfloat16
    )
    conv_out = jnp.einsum("bmd,bde->me", basis_in, bases, preferred_element_type=jnp.float32)
    normalizer = jnp.einsum("ihd,hd->ih", exp_query, ks_sum, precision=precise)
    attended = (
        jnp.einsum("ihd,hde->ihe", exp_query, kv_sum, precision=precise) / normalizer[:, :, None]
    )
    layer_out = attended.reshape(node_rows, feat_width) + conv_out
    coef_part = jnp.sum(aggregate[:, None] * basis_grad[None], axis=(2, 3))

    grad_heads = cotangent.reshape(node_rows, HEADS, HEAD_DIM)
    num_grad = grad_heads / normalizer[:, :, None]
    den_grad = -jnp.sum(grad_heads * attended, axis=2) / normalizer
    dkv_part = jnp.einsum("ihd,ihe->hde", exp_query, num_grad, precision=precise)
    dks_part = jnp.einsum("ihd,ih->hd", exp_query, den_grad, precision=precise)
    dks_size = dks_part.size
    reduced = group_sum(
        jnp.concatenate([dkv_part.reshape(-1), dks_part.reshape(-1), coef_part.reshape(-1)])
    )
    dkv_sum = reduced[:kv_size].reshape(dkv_part.shape)
    dks_sum = reduced[kv_size : kv_size + dks_size].reshape(dks_part.shape)
    coef_sum = reduced[kv_size + dks_size :].reshape(coef_part.shape)
    query_side = (
        jnp.einsum("ihe,hde->ihd", num_grad, kv_sum, precision=precise)
        + den_grad[:, :, None] * ks_sum[None]
    )
    key_side = jnp.einsum("ihe,hde->ihd", values, dkv_sum, precision=precise) + dks_sum[None]
    value_side = jnp.einsum("ihd,hde->ihe", exp_key, dkv_sum, precision=precise)
    proj_grad = jnp.concatenate(
        [
            (query_side * exp_query).reshape(node_rows, feat_width),
            (key_side * exp_key).reshape(node_rows, feat_width),
            value_side.reshape(node_rows, feat_width),
        ],
        axis=1,
    ).astype(jnp.bfloat16)
    grad_x = jnp.einsum("mc,dc->md", proj_grad, w_all, preferred_element_type=jnp.float32)
    returned = lax.all_to_all(
        table_grad[node_rows:].astype(jnp.bfloat16).reshape(peer_count, peer_slots, feat_width),
        "nodes",
        split_axis=0,
        concat_axis=0,
        tiled=True,
    )
    back_grad = jnp.einsum(
        "km,kd->md", pick, returned.reshape(-1, feat_width), preferred_element_type=jnp.float32
    )
    grad_x = grad_x + table_grad[:node_rows] + back_grad
    feat_part = jnp.einsum("mc,me->ce", features, proj_grad, preferred_element_type=jnp.float32)
    basis_part = jnp.einsum("bmc,me->cbe", basis_in, cot_half, preferred_element_type=jnp.float32)
    stacked = block_sum(jnp.concatenate([feat_part, basis_part.reshape(feat_width, -1)], axis=1))
    stacked = stacked * norm_scale
    query_grad = stacked[:, :feat_width]
    key_grad = stacked[:, feat_width : 2 * feat_width]
    value_grad = stacked[:, 2 * feat_width : 3 * feat_width]
    bases_grad = jnp.transpose(
        stacked[:, 3 * feat_width :].reshape(feat_width, basis_count, feat_width), (1, 0, 2)
    )
    coef_grad = coef_sum * norm_scale
    return (layer_out, grad_x, query_grad, key_grad, value_grad, bases_grad, coef_grad)


def solution(mesh):
    in_specs = (
        P(("outer", "nodes"), None),
        P(),
        P(),
        P(),
        P(),
        P(),
        P(("outer", "nodes"), None, None),
        P(("outer", "nodes"), None, None, None),
        P(("outer", "nodes"), None, None, None),
        P(("outer", "nodes"), None, None),
        P(("outer", "nodes"), None),
    )
    out_specs = (P(("outer", "nodes"), None), P(("outer", "nodes"), None), P(), P(), P(), P(), P())
    return jax.shard_map(
        per_device, mesh=mesh, in_specs=in_specs, out_specs=out_specs, check_vma=False
    )
```

```python
import math

import jax
import jax.numpy as jnp
from jax import lax
from jax.experimental import pallas as pl
from jax.experimental.pallas import tpu as pltpu
from jax.sharding import PartitionSpec as P

HEADS = 8
HEAD_DIM = 64
TILE = 128


precise = lax.Precision.HIGHEST
three_pass = lax.Precision.HIGH
NT = (((1,), (1,)), ((), ()))


def group_sum(flat):
    axes = ("outer", "nodes")
    devices = lax.axis_size("outer") * lax.axis_size("nodes")
    size = flat.shape[0]
    chunk = -(-size // (devices * 128)) * 128
    padded = jnp.pad(flat, (0, devices * chunk - size)).reshape(devices, chunk)
    received = lax.all_to_all(padded, axes, split_axis=0, concat_axis=0, tiled=True)
    mine = jnp.sum(received, axis=0, keepdims=True)
    spread = jnp.broadcast_to(mine, (devices, chunk))
    gathered = lax.all_to_all(spread, axes, split_axis=0, concat_axis=0, tiled=True)
    return gathered.reshape(-1)[:size]


def block_sum(block):
    axes = ("outer", "nodes")
    devices = lax.axis_size("outer") * lax.axis_size("nodes")
    rows, cols = block.shape
    parts = devices // (rows // 8)
    width = cols // parts
    tiles = block.reshape(rows // 8, 8, parts, width).transpose(0, 2, 1, 3)
    tiles = tiles.reshape(devices, 8, width)
    received = lax.all_to_all(tiles, axes, split_axis=0, concat_axis=0, tiled=True)
    mine = jnp.sum(received, axis=0, keepdims=True).astype(jnp.bfloat16)
    spread = jnp.broadcast_to(mine, (devices, 8, width))
    gathered = lax.all_to_all(spread, axes, split_axis=0, concat_axis=0, tiled=True)
    gathered = gathered.astype(jnp.float32).reshape(rows // 8, parts, 8, width).transpose(0, 2, 1, 3)
    return gathered.reshape(rows, cols)


def split_dot(a, b):
    a_hi = a.astype(jnp.bfloat16)
    a_lo = (a - a_hi.astype(jnp.float32)).astype(jnp.bfloat16)
    b_hi = b.astype(jnp.bfloat16)
    b_lo = (b - b_hi.astype(jnp.float32)).astype(jnp.bfloat16)
    out = jnp.dot(a_hi, b_hi, preferred_element_type=jnp.float32)
    out += jnp.dot(a_hi, b_lo, preferred_element_type=jnp.float32)
    out += jnp.dot(a_lo, b_hi, preferred_element_type=jnp.float32)
    return out


def graph_kernel(coef_ref, src_ref, dst_ref, cnt_ref, table_ref, grad_ref, agg_ref, tgrad_ref, wsum_ref):
    tile = pl.program_id(0)
    rel_count = src_ref.shape[0]
    table_rows = table_ref.shape[0]
    basis_count = grad_ref.shape[0]
    row_iota = lax.broadcasted_iota(jnp.int32, (table_rows, TILE), 0)
    node_iota = lax.broadcasted_iota(jnp.int32, (TILE, TILE), 0)
    slot_iota = lax.broadcasted_iota(jnp.int32, (TILE, TILE), 1)
    ones = jnp.ones((8, TILE), jnp.bfloat16)
    weights = [jnp.zeros((table_rows, TILE), jnp.float32) for _ in range(basis_count)]
    for r in range(rel_count):
        src_row = src_ref[r, 0]
        dst_row = dst_ref[r, 0]
        live = slot_iota < cnt_ref[r, tile]
        dst_t = ((node_iota == dst_row) & live).astype(jnp.bfloat16)
        src_t = (row_iota == src_row).astype(jnp.bfloat16)
        counts = lax.dot_general(dst_t, src_t, NT, preferred_element_type=jnp.float32)
        counts_t = lax.dot_general(src_t, dst_t, NT, preferred_element_type=jnp.float32)
        deg_col = jnp.maximum(jnp.sum(dst_t.astype(jnp.float32), axis=1, keepdims=True), 1.0)
        deg_row = jnp.maximum(
            lax.dot_general(ones, dst_t, NT, preferred_element_type=jnp.float32)[0:1], 1.0
        )
        sums = jnp.dot(counts.astype(jnp.bfloat16), table_ref[...], preferred_element_type=jnp.float32)
        agg_ref[r, 0] = sums / deg_col
        for b in range(basis_count):
            weights[b] = weights[b] + counts_t * (coef_ref[r, b] / deg_row)
    lanes = pl.ds(pl.multiple_of(tile * TILE, TILE), TILE)
    for b in range(basis_count):
        wsum_ref[b, :, lanes] = weights[b]

    @pl.when(tile == pl.num_programs(0) - 1)
    def _():
        total = split_dot(wsum_ref[0], grad_ref[0])
        for b in range(1, basis_count):
            total += split_dot(wsum_ref[b], grad_ref[b])
        tgrad_ref[...] = total


def graph_conv(rel_coef, src, dst, cnt, table, basis_grad):
    rel_count, tiles, slots = src.shape
    table_rows, width = table.shape
    basis_count, node_rows, _ = basis_grad.shape
    src4 = src.reshape(rel_count, tiles, 1, slots)
    dst4 = dst.reshape(rel_count, tiles, 1, slots)
    return pl.pallas_call(
        graph_kernel,
        grid=(tiles,),
        in_specs=[
            pl.BlockSpec(memory_space=pltpu.SMEM),
            pl.BlockSpec((rel_count, 1, 1, slots), lambda t: (0, t, 0, 0)),
            pl.BlockSpec((rel_count, 1, 1, slots), lambda t: (0, t, 0, 0)),
            pl.BlockSpec(memory_space=pltpu.SMEM),
            pl.BlockSpec((table_rows, width), lambda t: (0, 0)),
            pl.BlockSpec((basis_count, node_rows, width), lambda t: (0, 0, 0)),
        ],
        out_specs=[
            pl.BlockSpec((rel_count, 1, TILE, width), lambda t: (0, t, 0, 0)),
            pl.BlockSpec((table_rows, width), lambda t: (0, 0)),
        ],
        out_shape=[
            jax.ShapeDtypeStruct((rel_count, tiles, TILE, width), jnp.float32),
            jax.ShapeDtypeStruct((table_rows, width), jnp.float32),
        ],
        scratch_shapes=[pltpu.VMEM((basis_count, table_rows, node_rows), jnp.float32)],
        compiler_params=pltpu.CompilerParams(
            dimension_semantics=("arbitrary",), vmem_limit_bytes=64 * 1024 * 1024
        ),
    )(rel_coef, src4, dst4, cnt, table, basis_grad)


def per_device(
    features,
    w_query,
    w_key,
    w_value,
    bases,
    rel_coef,
    send_rows,
    tile_src,
    tile_dst,
    tile_count,
    cotangent,
):
    node_rows, feat_width = features.shape
    peer_count = lax.axis_size("nodes")
    total_nodes = node_rows * peer_count * lax.axis_size("outer")
    norm_scale = 1.0 / math.sqrt(total_nodes)
    basis_count = bases.shape[0]
    send_list = send_rows[0]
    peer_slots = send_list.shape[1]
    send_flat = send_list.reshape(-1)
    pick = (send_flat[:, None] == jnp.arange(node_rows)[None, :]).astype(jnp.bfloat16)
    outgoing = jnp.dot(pick, features, preferred_element_type=jnp.float32).astype(jnp.bfloat16)
    outgoing = outgoing.reshape(peer_count, peer_slots, feat_width)
    incoming = lax.all_to_all(outgoing, "nodes", split_axis=0, concat_axis=0, tiled=True)
    halo_table = jnp.concatenate([features, incoming.reshape(-1, feat_width)], axis=0)
    table_rows = halo_table.shape[0]

    w_all = jnp.concatenate([w_query, w_key, w_value], axis=1)
    projected = jnp.dot(features, w_all, preferred_element_type=jnp.float32)
    exp_query = jnp.exp(projected[:, :feat_width]).reshape(node_rows, HEADS, HEAD_DIM)
    exp_key = jnp.exp(projected[:, feat_width : 2 * feat_width]).reshape(node_rows, HEADS, HEAD_DIM)
    values = projected[:, 2 * feat_width :].reshape(node_rows, HEADS, HEAD_DIM)
    kv_part = jnp.einsum("ihd,ihe->hde", exp_key, values, precision=precise)
    ks_part = jnp.sum(exp_key, axis=0)
    kv_size = kv_part.size
    summary = group_sum(jnp.concatenate([kv_part.reshape(-1), ks_part.reshape(-1)]))
    kv_sum = summary[:kv_size].reshape(kv_part.shape)
    ks_sum = summary[kv_size:].reshape(ks_part.shape)

    cot_half = cotangent.astype(jnp.bfloat16)
    basis_grad = jnp.einsum("me,bde->bmd", cot_half, bases, preferred_element_type=jnp.float32)
    rel_count = tile_src.shape[1]
    aggregate, table_grad = graph_conv(
        rel_coef, tile_src[0], tile_dst[0], tile_count[0], halo_table, basis_grad
    )
    aggregate = aggregate.reshape(rel_count, node_rows, feat_width)
    basis_in = jnp.einsum("rb,rmd->bmd", rel_coef, aggregate, precision=precise).astype(
        jnp.bfloat16
    )
    conv_out = jnp.einsum("bmd,bde->me", basis_in, bases, preferred_element_type=jnp.float32)
    normalizer = jnp.einsum("ihd,hd->ih", exp_query, ks_sum, precision=precise)
    attended = (
        jnp.einsum("ihd,hde->ihe", exp_query, kv_sum, precision=precise) / normalizer[:, :, None]
    )
    layer_out = attended.reshape(node_rows, feat_width) + conv_out
    coef_part = jnp.sum(aggregate[:, None] * basis_grad[None], axis=(2, 3))

    grad_heads = cotangent.reshape(node_rows, HEADS, HEAD_DIM)
    num_grad = grad_heads / normalizer[:, :, None]
    den_grad = -jnp.sum(grad_heads * attended, axis=2) / normalizer
    dkv_part = jnp.einsum("ihd,ihe->hde", exp_query, num_grad, precision=precise)
    dks_part = jnp.einsum("ihd,ih->hd", exp_query, den_grad, precision=precise)
    dks_size = dks_part.size
    reduced = group_sum(
        jnp.concatenate([dkv_part.reshape(-1), dks_part.reshape(-1), coef_part.reshape(-1)])
    )
    dkv_sum = reduced[:kv_size].reshape(dkv_part.shape)
    dks_sum = reduced[kv_size : kv_size + dks_size].reshape(dks_part.shape)
    coef_sum = reduced[kv_size + dks_size :].reshape(coef_part.shape)
    query_side = (
        jnp.einsum("ihe,hde->ihd", num_grad, kv_sum, precision=precise)
        + den_grad[:, :, None] * ks_sum[None]
    )
    key_side = jnp.einsum("ihe,hde->ihd", values, dkv_sum, precision=precise) + dks_sum[None]
    value_side = jnp.einsum("ihd,hde->ihe", exp_key, dkv_sum, precision=precise)
    proj_grad = jnp.concatenate(
        [
            (query_side * exp_query).reshape(node_rows, feat_width),
            (key_side * exp_key).reshape(node_rows, feat_width),
            value_side.reshape(node_rows, feat_width),
        ],
        axis=1,
    ).astype(jnp.bfloat16)
    grad_x = jnp.einsum("mc,dc->md", proj_grad, w_all, preferred_element_type=jnp.float32)
    returned = lax.all_to_all(
        table_grad[node_rows:].astype(jnp.bfloat16).reshape(peer_count, peer_slots, feat_width),
        "nodes",
        split_axis=0,
        concat_axis=0,
        tiled=True,
    )
    back_grad = jnp.einsum(
        "km,kd->md", pick, returned.reshape(-1, feat_width), preferred_element_type=jnp.float32
    )
    grad_x = grad_x + table_grad[:node_rows] + back_grad
    feat_part = jnp.einsum("mc,me->ce", features, proj_grad, preferred_element_type=jnp.float32)
    basis_part = jnp.einsum("bmc,me->cbe", basis_in, cot_half, preferred_element_type=jnp.float32)
    stacked = block_sum(jnp.concatenate([feat_part, basis_part.reshape(feat_width, -1)], axis=1))
    stacked = stacked * norm_scale
    query_grad = stacked[:, :feat_width]
    key_grad = stacked[:, feat_width : 2 * feat_width]
    value_grad = stacked[:, 2 * feat_width : 3 * feat_width]
    bases_grad = jnp.transpose(
        stacked[:, 3 * feat_width :].reshape(feat_width, basis_count, feat_width), (1, 0, 2)
    )
    coef_grad = coef_sum * norm_scale
    return (layer_out, grad_x, query_grad, key_grad, value_grad, bases_grad, coef_grad)


def solution(mesh):
    in_specs = (
        P(("outer", "nodes"), None),
        P(),
        P(),
        P(),
        P(),
        P(),
        P(("outer", "nodes"), None, None),
        P(("outer", "nodes"), None, None, None),
        P(("outer", "nodes"), None, None, None),
        P(("outer", "nodes"), None, None),
        P(("outer", "nodes"), None),
    )
    out_specs = (P(("outer", "nodes"), None), P(("outer", "nodes"), None), P(), P(), P(), P(), P())
    return jax.shard_map(
        per_device, mesh=mesh, in_specs=in_specs, out_specs=out_specs, check_vma=False
    )
```

```python
import math

import jax
import jax.numpy as jnp
from jax import lax
from jax.experimental import pallas as pl
from jax.experimental.pallas import tpu as pltpu
from jax.sharding import PartitionSpec as P

HEADS = 8
HEAD_DIM = 64
TILE = 128


precise = lax.Precision.HIGHEST
three_pass = lax.Precision.HIGH
NT = (((1,), (1,)), ((), ()))


def group_sum(flat, hold=None):
    axes = ("outer", "nodes")
    devices = lax.axis_size("outer") * lax.axis_size("nodes")
    size = flat.shape[0]
    chunk = -(-size // (devices * 128)) * 128
    padded = jnp.pad(flat, (0, devices * chunk - size)).reshape(devices, chunk)
    received = lax.all_to_all(padded, axes, split_axis=0, concat_axis=0, tiled=True)
    if hold is not None:
        received, hold = lax.optimization_barrier((received, hold))
    mine = jnp.sum(received, axis=0, keepdims=True)
    spread = jnp.broadcast_to(mine, (devices, chunk))
    gathered = lax.all_to_all(spread, axes, split_axis=0, concat_axis=0, tiled=True)
    if hold is not None:
        return gathered.reshape(-1)[:size], hold
    return gathered.reshape(-1)[:size]


def block_sum(block):
    axes = ("outer", "nodes")
    devices = lax.axis_size("outer") * lax.axis_size("nodes")
    rows, cols = block.shape
    parts = devices // (rows // 8)
    width = cols // parts
    tiles = block.reshape(rows // 8, 8, parts, width).transpose(0, 2, 1, 3)
    tiles = tiles.reshape(devices, 8, width)
    received = lax.all_to_all(tiles, axes, split_axis=0, concat_axis=0, tiled=True)
    mine = jnp.sum(received, axis=0, keepdims=True).astype(jnp.bfloat16)
    spread = jnp.broadcast_to(mine, (devices, 8, width))
    gathered = lax.all_to_all(spread, axes, split_axis=0, concat_axis=0, tiled=True)
    gathered = gathered.astype(jnp.float32).reshape(rows // 8, parts, 8, width).transpose(0, 2, 1, 3)
    return gathered.reshape(rows, cols)


def split_dot(a, b):
    a_hi = a.astype(jnp.bfloat16)
    a_lo = (a - a_hi.astype(jnp.float32)).astype(jnp.bfloat16)
    b_hi = b.astype(jnp.bfloat16)
    b_lo = (b - b_hi.astype(jnp.float32)).astype(jnp.bfloat16)
    out = jnp.dot(a_hi, b_hi, preferred_element_type=jnp.float32)
    out += jnp.dot(a_hi, b_lo, preferred_element_type=jnp.float32)
    out += jnp.dot(a_lo, b_hi, preferred_element_type=jnp.float32)
    return out


def graph_kernel(coef_ref, src_ref, dst_ref, cnt_ref, table_ref, grad_ref, agg_ref, tgrad_ref, wsum_ref):
    tile = pl.program_id(0)
    rel_count = src_ref.shape[0]
    table_rows = table_ref.shape[0]
    basis_count = grad_ref.shape[0]
    row_iota = lax.broadcasted_iota(jnp.int32, (table_rows, TILE), 0)
    node_iota = lax.broadcasted_iota(jnp.int32, (TILE, TILE), 0)
    slot_iota = lax.broadcasted_iota(jnp.int32, (TILE, TILE), 1)
    ones = jnp.ones((8, TILE), jnp.bfloat16)
    weights = [jnp.zeros((table_rows, TILE), jnp.float32) for _ in range(basis_count)]
    for r in range(rel_count):
        src_row = src_ref[r, 0]
        dst_row = dst_ref[r, 0]
        live = slot_iota < cnt_ref[r, tile]
        dst_t = ((node_iota == dst_row) & live).astype(jnp.bfloat16)
        src_t = (row_iota == src_row).astype(jnp.bfloat16)
        counts = lax.dot_general(dst_t, src_t, NT, preferred_element_type=jnp.float32)
        counts_t = lax.dot_general(src_t, dst_t, NT, preferred_element_type=jnp.float32)
        deg_col = jnp.maximum(jnp.sum(dst_t.astype(jnp.float32), axis=1, keepdims=True), 1.0)
        deg_row = jnp.maximum(
            lax.dot_general(ones, dst_t, NT, preferred_element_type=jnp.float32)[0:1], 1.0
        )
        sums = jnp.dot(counts.astype(jnp.bfloat16), table_ref[...], preferred_element_type=jnp.float32)
        agg_ref[r, 0] = sums / deg_col
        for b in range(basis_count):
            weights[b] = weights[b] + counts_t * (coef_ref[r, b] / deg_row)
    lanes = pl.ds(pl.multiple_of(tile * TILE, TILE), TILE)
    for b in range(basis_count):
        wsum_ref[b, :, lanes] = weights[b]

    @pl.when(tile == pl.num_programs(0) - 1)
    def _():
        total = split_dot(wsum_ref[0], grad_ref[0])
        for b in range(1, basis_count):
            total += split_dot(wsum_ref[b], grad_ref[b])
        tgrad_ref[...] = total


def graph_conv(rel_coef, src, dst, cnt, table, basis_grad):
    rel_count, tiles, slots = src.shape
    table_rows, width = table.shape
    basis_count, node_rows, _ = basis_grad.shape
    src4 = src.reshape(rel_count, tiles, 1, slots)
    dst4 = dst.reshape(rel_count, tiles, 1, slots)
    return pl.pallas_call(
        graph_kernel,
        grid=(tiles,),
        in_specs=[
            pl.BlockSpec(memory_space=pltpu.SMEM),
            pl.BlockSpec((rel_count, 1, 1, slots), lambda t: (0, t, 0, 0)),
            pl.BlockSpec((rel_count, 1, 1, slots), lambda t: (0, t, 0, 0)),
            pl.BlockSpec(memory_space=pltpu.SMEM),
            pl.BlockSpec((table_rows, width), lambda t: (0, 0)),
            pl.BlockSpec((basis_count, node_rows, width), lambda t: (0, 0, 0)),
        ],
        out_specs=[
            pl.BlockSpec((rel_count, 1, TILE, width), lambda t: (0, t, 0, 0)),
            pl.BlockSpec((table_rows, width), lambda t: (0, 0)),
        ],
        out_shape=[
            jax.ShapeDtypeStruct((rel_count, tiles, TILE, width), jnp.float32),
            jax.ShapeDtypeStruct((table_rows, width), jnp.float32),
        ],
        scratch_shapes=[pltpu.VMEM((basis_count, table_rows, node_rows), jnp.float32)],
        compiler_params=pltpu.CompilerParams(
            dimension_semantics=("arbitrary",), vmem_limit_bytes=64 * 1024 * 1024
        ),
        cost_estimate=pl.CostEstimate(
            flops=2 * rel_count * tiles * TILE * table_rows * (2 * TILE + width)
            + 6 * basis_count * table_rows * node_rows * width,
            bytes_accessed=table.size * 2 + basis_grad.size * 4 + 4 * width * (
                rel_count * tiles * TILE + table_rows
            ),
            transcendentals=0,
        ),
    )(rel_coef, src4, dst4, cnt, table, basis_grad)


def per_device(
    features,
    w_query,
    w_key,
    w_value,
    bases,
    rel_coef,
    send_rows,
    tile_src,
    tile_dst,
    tile_count,
    cotangent,
):
    node_rows, feat_width = features.shape
    peer_count = lax.axis_size("nodes")
    total_nodes = node_rows * peer_count * lax.axis_size("outer")
    norm_scale = 1.0 / math.sqrt(total_nodes)
    basis_count = bases.shape[0]
    send_list = send_rows[0]
    peer_slots = send_list.shape[1]
    send_flat = send_list.reshape(-1)
    pick = (send_flat[:, None] == jnp.arange(node_rows)[None, :]).astype(jnp.bfloat16)
    outgoing = jnp.dot(pick, features, preferred_element_type=jnp.float32).astype(jnp.bfloat16)
    outgoing = outgoing.reshape(peer_count, peer_slots, feat_width)
    incoming = lax.all_to_all(outgoing, "nodes", split_axis=0, concat_axis=0, tiled=True)
    halo_table = jnp.concatenate([features, incoming.reshape(-1, feat_width)], axis=0)
    table_rows = halo_table.shape[0]

    w_all = jnp.concatenate([w_query, w_key, w_value], axis=1)
    projected = jnp.dot(features, w_all, preferred_element_type=jnp.float32)
    exp_query = jnp.exp(projected[:, :feat_width]).reshape(node_rows, HEADS, HEAD_DIM)
    exp_key = jnp.exp(projected[:, feat_width : 2 * feat_width]).reshape(node_rows, HEADS, HEAD_DIM)
    values = projected[:, 2 * feat_width :].reshape(node_rows, HEADS, HEAD_DIM)
    kv_part = jnp.einsum("ihd,ihe->hde", exp_key, values, precision=precise)
    ks_part = jnp.sum(exp_key, axis=0)
    kv_size = kv_part.size
    cot_half = cotangent.astype(jnp.bfloat16)
    basis_grad = jnp.einsum("me,bde->bmd", cot_half, bases, preferred_element_type=jnp.float32)
    rel_count = tile_src.shape[1]
    summary_part, halo_table = lax.optimization_barrier(
        (jnp.concatenate([kv_part.reshape(-1), ks_part.reshape(-1)]), halo_table)
    )
    aggregate, table_grad = graph_conv(
        rel_coef, tile_src[0], tile_dst[0], tile_count[0], halo_table, basis_grad
    )
    aggregate = aggregate.reshape(rel_count, node_rows, feat_width)
    summary, (aggregate, table_grad) = group_sum(summary_part, (aggregate, table_grad))
    kv_sum = summary[:kv_size].reshape(kv_part.shape)
    ks_sum = summary[kv_size:].reshape(ks_part.shape)

    basis_in = jnp.einsum("rb,rmd->bmd", rel_coef, aggregate, precision=precise).astype(
        jnp.bfloat16
    )
    conv_out = jnp.einsum("bmd,bde->me", basis_in, bases, preferred_element_type=jnp.float32)
    normalizer = jnp.einsum("ihd,hd->ih", exp_query, ks_sum, precision=precise)
    attended = (
        jnp.einsum("ihd,hde->ihe", exp_query, kv_sum, precision=precise) / normalizer[:, :, None]
    )
    layer_out = attended.reshape(node_rows, feat_width) + conv_out
    coef_part = jnp.sum(aggregate[:, None] * basis_grad[None], axis=(2, 3))

    grad_heads = cotangent.reshape(node_rows, HEADS, HEAD_DIM)
    num_grad = grad_heads / normalizer[:, :, None]
    den_grad = -jnp.sum(grad_heads * attended, axis=2) / normalizer
    dkv_part = jnp.einsum("ihd,ihe->hde", exp_query, num_grad, precision=precise)
    dks_part = jnp.einsum("ihd,ih->hd", exp_query, den_grad, precision=precise)
    dks_size = dks_part.size
    reduced = group_sum(
        jnp.concatenate([dkv_part.reshape(-1), dks_part.reshape(-1), coef_part.reshape(-1)])
    )
    dkv_sum = reduced[:kv_size].reshape(dkv_part.shape)
    dks_sum = reduced[kv_size : kv_size + dks_size].reshape(dks_part.shape)
    coef_sum = reduced[kv_size + dks_size :].reshape(coef_part.shape)
    query_side = (
        jnp.einsum("ihe,hde->ihd", num_grad, kv_sum, precision=precise)
        + den_grad[:, :, None] * ks_sum[None]
    )
    key_side = jnp.einsum("ihe,hde->ihd", values, dkv_sum, precision=precise) + dks_sum[None]
    value_side = jnp.einsum("ihd,hde->ihe", exp_key, dkv_sum, precision=precise)
    proj_grad = jnp.concatenate(
        [
            (query_side * exp_query).reshape(node_rows, feat_width),
            (key_side * exp_key).reshape(node_rows, feat_width),
            value_side.reshape(node_rows, feat_width),
        ],
        axis=1,
    ).astype(jnp.bfloat16)
    grad_x = jnp.einsum("mc,dc->md", proj_grad, w_all, preferred_element_type=jnp.float32)
    returned = lax.all_to_all(
        table_grad[node_rows:].astype(jnp.bfloat16).reshape(peer_count, peer_slots, feat_width),
        "nodes",
        split_axis=0,
        concat_axis=0,
        tiled=True,
    )
    back_grad = jnp.einsum(
        "km,kd->md", pick, returned.reshape(-1, feat_width), preferred_element_type=jnp.float32
    )
    grad_x = grad_x + table_grad[:node_rows] + back_grad
    feat_part = jnp.einsum("mc,me->ce", features, proj_grad, preferred_element_type=jnp.float32)
    basis_part = jnp.einsum("bmc,me->cbe", basis_in, cot_half, preferred_element_type=jnp.float32)
    stacked = block_sum(jnp.concatenate([feat_part, basis_part.reshape(feat_width, -1)], axis=1))
    stacked = stacked * norm_scale
    query_grad = stacked[:, :feat_width]
    key_grad = stacked[:, feat_width : 2 * feat_width]
    value_grad = stacked[:, 2 * feat_width : 3 * feat_width]
    bases_grad = jnp.transpose(
        stacked[:, 3 * feat_width :].reshape(feat_width, basis_count, feat_width), (1, 0, 2)
    )
    coef_grad = coef_sum * norm_scale
    return (layer_out, grad_x, query_grad, key_grad, value_grad, bases_grad, coef_grad)


def solution(mesh):
    in_specs = (
        P(("outer", "nodes"), None),
        P(),
        P(),
        P(),
        P(),
        P(),
        P(("outer", "nodes"), None, None),
        P(("outer", "nodes"), None, None, None),
        P(("outer", "nodes"), None, None, None),
        P(("outer", "nodes"), None, None),
        P(("outer", "nodes"), None),
    )
    out_specs = (P(("outer", "nodes"), None), P(("outer", "nodes"), None), P(), P(), P(), P(), P())
    return jax.shard_map(
        per_device, mesh=mesh, in_specs=in_specs, out_specs=out_specs, check_vma=False
    )
```

```python
import math

import jax
import jax.numpy as jnp
from jax import lax
from jax.experimental import pallas as pl
from jax.experimental.pallas import tpu as pltpu
from jax.sharding import PartitionSpec as P

HEADS = 8
HEAD_DIM = 64
TILE = 128


precise = lax.Precision.HIGHEST
three_pass = lax.Precision.HIGH
NT = (((1,), (1,)), ((), ()))


def group_sum(flat):
    axes = ("outer", "nodes")
    devices = lax.axis_size("outer") * lax.axis_size("nodes")
    size = flat.shape[0]
    chunk = -(-size // (devices * 128)) * 128
    padded = jnp.pad(flat, (0, devices * chunk - size)).reshape(devices, chunk)
    received = lax.all_to_all(padded, axes, split_axis=0, concat_axis=0, tiled=True)
    mine = jnp.sum(received, axis=0, keepdims=True)
    spread = jnp.broadcast_to(mine, (devices, chunk))
    gathered = lax.all_to_all(spread, axes, split_axis=0, concat_axis=0, tiled=True)
    return gathered.reshape(-1)[:size]


def block_sum(block):
    axes = ("outer", "nodes")
    devices = lax.axis_size("outer") * lax.axis_size("nodes")
    rows, cols = block.shape
    parts = devices // (rows // 8)
    width = cols // parts
    tiles = block.reshape(rows // 8, 8, parts, width).transpose(0, 2, 1, 3)
    tiles = tiles.reshape(devices, 8, width)
    received = lax.all_to_all(tiles, axes, split_axis=0, concat_axis=0, tiled=True)
    mine = jnp.sum(received, axis=0, keepdims=True).astype(jnp.bfloat16)
    spread = jnp.broadcast_to(mine, (devices, 8, width))
    gathered = lax.all_to_all(spread, axes, split_axis=0, concat_axis=0, tiled=True)
    gathered = gathered.astype(jnp.float32).reshape(rows // 8, parts, 8, width).transpose(0, 2, 1, 3)
    return gathered.reshape(rows, cols)


def split_dot(a, b):
    a_hi = a.astype(jnp.bfloat16)
    a_lo = (a - a_hi.astype(jnp.float32)).astype(jnp.bfloat16)
    b_hi = b.astype(jnp.bfloat16)
    b_lo = (b - b_hi.astype(jnp.float32)).astype(jnp.bfloat16)
    out = jnp.dot(a_hi, b_hi, preferred_element_type=jnp.float32)
    out += jnp.dot(a_hi, b_lo, preferred_element_type=jnp.float32)
    out += jnp.dot(a_lo, b_hi, preferred_element_type=jnp.float32)
    return out


def graph_kernel(coef_ref, src_ref, dst_ref, cnt_ref, table_ref, grad_ref, agg_ref, tgrad_ref, wsum_ref):
    tile = pl.program_id(0)
    rel_count = src_ref.shape[0]
    table_rows = table_ref.shape[0]
    basis_count = grad_ref.shape[0]
    row_iota = lax.broadcasted_iota(jnp.int32, (table_rows, TILE), 0)
    node_iota = lax.broadcasted_iota(jnp.int32, (TILE, TILE), 0)
    slot_iota = lax.broadcasted_iota(jnp.int32, (TILE, TILE), 1)
    ones = jnp.ones((8, TILE), jnp.bfloat16)
    weights = [jnp.zeros((table_rows, TILE), jnp.float32) for _ in range(basis_count)]
    for r in range(rel_count):
        src_row = src_ref[r, 0]
        dst_row = dst_ref[r, 0]
        live = slot_iota < cnt_ref[r, tile]
        dst_t = ((node_iota == dst_row) & live).astype(jnp.bfloat16)
        src_t = (row_iota == src_row).astype(jnp.bfloat16)
        counts = lax.dot_general(dst_t, src_t, NT, preferred_element_type=jnp.float32)
        counts_t = lax.dot_general(src_t, dst_t, NT, preferred_element_type=jnp.float32)
        deg_col = jnp.maximum(jnp.sum(dst_t.astype(jnp.float32), axis=1, keepdims=True), 1.0)
        deg_row = jnp.maximum(
            lax.dot_general(ones, dst_t, NT, preferred_element_type=jnp.float32)[0:1], 1.0
        )
        sums = jnp.dot(counts.astype(jnp.bfloat16), table_ref[...], preferred_element_type=jnp.float32)
        agg_ref[r, 0] = sums / deg_col
        for b in range(basis_count):
            weights[b] = weights[b] + counts_t * (coef_ref[r, b] / deg_row)
    lanes = pl.ds(pl.multiple_of(tile * TILE, TILE), TILE)
    for b in range(basis_count):
        wsum_ref[b, :, lanes] = weights[b]

    @pl.when(tile == pl.num_programs(0) - 1)
    def _():
        total = split_dot(wsum_ref[0], grad_ref[0])
        for b in range(1, basis_count):
            total += split_dot(wsum_ref[b], grad_ref[b])
        tgrad_ref[...] = total


def graph_conv(rel_coef, src, dst, cnt, table, basis_grad):
    rel_count, tiles, slots = src.shape
    table_rows, width = table.shape
    basis_count, node_rows, _ = basis_grad.shape
    src4 = src.reshape(rel_count, tiles, 1, slots)
    dst4 = dst.reshape(rel_count, tiles, 1, slots)
    return pl.pallas_call(
        graph_kernel,
        grid=(tiles,),
        in_specs=[
            pl.BlockSpec(memory_space=pltpu.SMEM),
            pl.BlockSpec((rel_count, 1, 1, slots), lambda t: (0, t, 0, 0)),
            pl.BlockSpec((rel_count, 1, 1, slots), lambda t: (0, t, 0, 0)),
            pl.BlockSpec(memory_space=pltpu.SMEM),
            pl.BlockSpec((table_rows, width), lambda t: (0, 0)),
            pl.BlockSpec((basis_count, node_rows, width), lambda t: (0, 0, 0)),
        ],
        out_specs=[
            pl.BlockSpec((rel_count, 1, TILE, width), lambda t: (0, t, 0, 0)),
            pl.BlockSpec((table_rows, width), lambda t: (0, 0)),
        ],
        out_shape=[
            jax.ShapeDtypeStruct((rel_count, tiles, TILE, width), jnp.float32),
            jax.ShapeDtypeStruct((table_rows, width), jnp.float32),
        ],
        scratch_shapes=[pltpu.VMEM((basis_count, table_rows, node_rows), jnp.float32)],
        compiler_params=pltpu.CompilerParams(
            dimension_semantics=("arbitrary",), vmem_limit_bytes=64 * 1024 * 1024
        ),
    )(rel_coef, src4, dst4, cnt, table, basis_grad)


def per_device(
    features,
    w_query,
    w_key,
    w_value,
    bases,
    rel_coef,
    send_rows,
    tile_src,
    tile_dst,
    tile_count,
    cotangent,
):
    node_rows, feat_width = features.shape
    peer_count = lax.axis_size("nodes")
    total_nodes = node_rows * peer_count * lax.axis_size("outer")
    norm_scale = 1.0 / math.sqrt(total_nodes)
    basis_count = bases.shape[0]
    send_list = send_rows[0]
    peer_slots = send_list.shape[1]
    send_flat = send_list.reshape(-1)
    pick = (send_flat[:, None] == jnp.arange(node_rows)[None, :]).astype(jnp.bfloat16)
    outgoing = jnp.dot(pick, features, preferred_element_type=jnp.float32).astype(jnp.bfloat16)
    outgoing = outgoing.reshape(peer_count, peer_slots, feat_width)
    incoming = lax.all_to_all(outgoing, "nodes", split_axis=0, concat_axis=0, tiled=True)
    halo_table = jnp.concatenate([features, incoming.reshape(-1, feat_width)], axis=0)
    table_rows = halo_table.shape[0]

    w_all = jnp.concatenate([w_query, w_key, w_value], axis=1)
    projected = jnp.dot(features, w_all, preferred_element_type=jnp.float32)
    exp_query = jnp.exp(projected[:, :feat_width]).reshape(node_rows, HEADS, HEAD_DIM)
    exp_key = jnp.exp(projected[:, feat_width : 2 * feat_width]).reshape(node_rows, HEADS, HEAD_DIM)
    values = projected[:, 2 * feat_width :].reshape(node_rows, HEADS, HEAD_DIM)
    kv_part = jnp.einsum("ihd,ihe->hde", exp_key, values, precision=precise)
    ks_part = jnp.sum(exp_key, axis=0)
    kv_size = kv_part.size
    summary = group_sum(jnp.concatenate([kv_part.reshape(-1), ks_part.reshape(-1)]))
    kv_sum = summary[:kv_size].reshape(kv_part.shape)
    ks_sum = summary[kv_size:].reshape(ks_part.shape)

    cot_half = cotangent.astype(jnp.bfloat16)
    basis_grad = jnp.einsum("me,bde->bmd", cot_half, bases, preferred_element_type=jnp.float32)
    rel_count = tile_src.shape[1]
    aggregate, table_grad = graph_conv(
        rel_coef, tile_src[0], tile_dst[0], tile_count[0], halo_table, basis_grad
    )
    aggregate = aggregate.reshape(rel_count, node_rows, feat_width)
    basis_in = jnp.einsum("rb,rmd->bmd", rel_coef, aggregate, precision=precise).astype(
        jnp.bfloat16
    )
    conv_out = jnp.einsum("bmd,bde->me", basis_in, bases, preferred_element_type=jnp.float32)
    normalizer = jnp.einsum("ihd,hd->ih", exp_query, ks_sum, precision=precise)
    attended = (
        jnp.einsum("ihd,hde->ihe", exp_query, kv_sum, precision=precise) / normalizer[:, :, None]
    )
    layer_out = attended.reshape(node_rows, feat_width) + conv_out
    coef_part = jnp.sum(aggregate[:, None] * basis_grad[None], axis=(2, 3))

    grad_heads = cotangent.reshape(node_rows, HEADS, HEAD_DIM)
    num_grad = grad_heads / normalizer[:, :, None]
    den_grad = -jnp.sum(grad_heads * attended, axis=2) / normalizer
    dkv_part = jnp.einsum("ihd,ihe->hde", exp_query, num_grad, precision=precise)
    dks_part = jnp.einsum("ihd,ih->hd", exp_query, den_grad, precision=precise)
    dks_size = dks_part.size
    reduced = group_sum(
        jnp.concatenate([dkv_part.reshape(-1), dks_part.reshape(-1), coef_part.reshape(-1)])
    )
    dkv_sum = reduced[:kv_size].reshape(dkv_part.shape)
    dks_sum = reduced[kv_size : kv_size + dks_size].reshape(dks_part.shape)
    coef_flat = lax.optimization_barrier(reduced[kv_size + dks_size :])
    coef_sum = coef_flat.reshape(coef_part.shape)
    query_side = (
        jnp.einsum("ihe,hde->ihd", num_grad, kv_sum, precision=precise)
        + den_grad[:, :, None] * ks_sum[None]
    )
    key_side = jnp.einsum("ihe,hde->ihd", values, dkv_sum, precision=precise) + dks_sum[None]
    value_side = jnp.einsum("ihd,hde->ihe", exp_key, dkv_sum, precision=precise)
    proj_grad = jnp.concatenate(
        [
            (query_side * exp_query).reshape(node_rows, feat_width),
            (key_side * exp_key).reshape(node_rows, feat_width),
            value_side.reshape(node_rows, feat_width),
        ],
        axis=1,
    ).astype(jnp.bfloat16)
    grad_x = jnp.einsum("mc,dc->md", proj_grad, w_all, preferred_element_type=jnp.float32)
    returned = lax.all_to_all(
        table_grad[node_rows:].astype(jnp.bfloat16).reshape(peer_count, peer_slots, feat_width),
        "nodes",
        split_axis=0,
        concat_axis=0,
        tiled=True,
    )
    back_grad = jnp.einsum(
        "km,kd->md", pick, returned.reshape(-1, feat_width), preferred_element_type=jnp.float32
    )
    grad_x = grad_x + table_grad[:node_rows] + back_grad
    feat_part = jnp.einsum("mc,me->ce", features, proj_grad, preferred_element_type=jnp.float32)
    basis_part = jnp.einsum("bmc,me->cbe", basis_in, cot_half, preferred_element_type=jnp.float32)
    stacked = block_sum(jnp.concatenate([feat_part, basis_part.reshape(feat_width, -1)], axis=1))
    stacked = stacked * norm_scale
    query_grad = stacked[:, :feat_width]
    key_grad = stacked[:, feat_width : 2 * feat_width]
    value_grad = stacked[:, 2 * feat_width : 3 * feat_width]
    bases_grad = jnp.transpose(
        stacked[:, 3 * feat_width :].reshape(feat_width, basis_count, feat_width), (1, 0, 2)
    )
    coef_grad = coef_sum * norm_scale
    return (layer_out, grad_x, query_grad, key_grad, value_grad, bases_grad, coef_grad)


def solution(mesh):
    in_specs = (
        P(("outer", "nodes"), None),
        P(),
        P(),
        P(),
        P(),
        P(),
        P(("outer", "nodes"), None, None),
        P(("outer", "nodes"), None, None, None),
        P(("outer", "nodes"), None, None, None),
        P(("outer", "nodes"), None, None),
        P(("outer", "nodes"), None),
    )
    out_specs = (P(("outer", "nodes"), None), P(("outer", "nodes"), None), P(), P(), P(), P(), P())
    return jax.shard_map(
        per_device, mesh=mesh, in_specs=in_specs, out_specs=out_specs, check_vma=False
    )
```

```python
import math

import jax
import jax.numpy as jnp
from jax import lax
from jax.experimental import pallas as pl
from jax.experimental.pallas import tpu as pltpu
from jax.sharding import PartitionSpec as P

HEADS = 8
HEAD_DIM = 64
TILE = 128


precise = lax.Precision.HIGHEST
three_pass = lax.Precision.HIGH
NT = (((1,), (1,)), ((), ()))


def group_sum(flat):
    axes = ("outer", "nodes")
    devices = lax.axis_size("outer") * lax.axis_size("nodes")
    size = flat.shape[0]
    chunk = -(-size // (devices * 128)) * 128
    padded = jnp.pad(flat, (0, devices * chunk - size)).reshape(devices, chunk)
    received = lax.all_to_all(padded, axes, split_axis=0, concat_axis=0, tiled=True)
    mine = jnp.sum(received, axis=0, keepdims=True)
    spread = jnp.broadcast_to(mine, (devices, chunk))
    gathered = lax.all_to_all(spread, axes, split_axis=0, concat_axis=0, tiled=True)
    return gathered.reshape(-1)[:size]


def block_sum(block):
    axes = ("outer", "nodes")
    devices = lax.axis_size("outer") * lax.axis_size("nodes")
    rows, cols = block.shape
    parts = devices // (rows // 8)
    width = cols // parts
    tiles = block.reshape(rows // 8, 8, parts, width).transpose(0, 2, 1, 3)
    tiles = tiles.reshape(devices, 8, width)
    received = lax.all_to_all(tiles, axes, split_axis=0, concat_axis=0, tiled=True)
    mine = jnp.sum(received, axis=0, keepdims=True).astype(jnp.bfloat16)
    spread = jnp.broadcast_to(mine, (devices, 8, width))
    gathered = lax.all_to_all(spread, axes, split_axis=0, concat_axis=0, tiled=True)
    gathered = gathered.astype(jnp.float32).reshape(rows // 8, parts, 8, width).transpose(0, 2, 1, 3)
    return gathered.reshape(rows, cols)


def graph_kernel(coef_ref, src_ref, dst_ref, cnt_ref, table_ref, agg_ref, wsum_ref):
    tile = pl.program_id(0)
    rel_count = src_ref.shape[0]
    table_rows = table_ref.shape[0]
    basis_count = wsum_ref.shape[0]
    row_iota = lax.broadcasted_iota(jnp.int32, (table_rows, TILE), 0)
    node_iota = lax.broadcasted_iota(jnp.int32, (TILE, TILE), 0)
    slot_iota = lax.broadcasted_iota(jnp.int32, (TILE, TILE), 1)
    ones = jnp.ones((8, TILE), jnp.bfloat16)
    weights = [jnp.zeros((table_rows, TILE), jnp.float32) for _ in range(basis_count)]
    for r in range(rel_count):
        src_row = src_ref[r, 0]
        dst_row = dst_ref[r, 0]
        live = slot_iota < cnt_ref[r, tile]
        dst_t = ((node_iota == dst_row) & live).astype(jnp.bfloat16)
        src_t = (row_iota == src_row).astype(jnp.bfloat16)
        counts = lax.dot_general(dst_t, src_t, NT, preferred_element_type=jnp.float32)
        counts_t = lax.dot_general(src_t, dst_t, NT, preferred_element_type=jnp.float32)
        deg_col = jnp.maximum(jnp.sum(dst_t.astype(jnp.float32), axis=1, keepdims=True), 1.0)
        deg_row = jnp.maximum(
            lax.dot_general(ones, dst_t, NT, preferred_element_type=jnp.float32)[0:1], 1.0
        )
        sums = jnp.dot(counts.astype(jnp.bfloat16), table_ref[...], preferred_element_type=jnp.float32)
        agg_ref[r, 0] = sums / deg_col
        for b in range(basis_count):
            weights[b] = weights[b] + counts_t * (coef_ref[r, b] / deg_row)
    for b in range(basis_count):
        wsum_ref[b] = weights[b]


def graph_conv(rel_coef, src, dst, cnt, table, basis_count):
    rel_count, tiles, slots = src.shape
    table_rows, width = table.shape
    src4 = src.reshape(rel_count, tiles, 1, slots)
    dst4 = dst.reshape(rel_count, tiles, 1, slots)
    return pl.pallas_call(
        graph_kernel,
        grid=(tiles,),
        in_specs=[
            pl.BlockSpec(memory_space=pltpu.SMEM),
            pl.BlockSpec((rel_count, 1, 1, slots), lambda t: (0, t, 0, 0)),
            pl.BlockSpec((rel_count, 1, 1, slots), lambda t: (0, t, 0, 0)),
            pl.BlockSpec(memory_space=pltpu.SMEM),
            pl.BlockSpec((table_rows, width), lambda t: (0, 0)),
        ],
        out_specs=[
            pl.BlockSpec((rel_count, 1, TILE, width), lambda t: (0, t, 0, 0)),
            pl.BlockSpec((basis_count, table_rows, TILE), lambda t: (0, 0, t)),
        ],
        out_shape=[
            jax.ShapeDtypeStruct((rel_count, tiles, TILE, width), jnp.float32),
            jax.ShapeDtypeStruct((basis_count, table_rows, tiles * TILE), jnp.float32),
        ],
        compiler_params=pltpu.CompilerParams(
            dimension_semantics=("parallel",), vmem_limit_bytes=64 * 1024 * 1024
        ),
    )(rel_coef, src4, dst4, cnt, table)


def per_device(
    features,
    w_query,
    w_key,
    w_value,
    bases,
    rel_coef,
    send_rows,
    tile_src,
    tile_dst,
    tile_count,
    cotangent,
):
    node_rows, feat_width = features.shape
    peer_count = lax.axis_size("nodes")
    total_nodes = node_rows * peer_count * lax.axis_size("outer")
    norm_scale = 1.0 / math.sqrt(total_nodes)
    basis_count = bases.shape[0]
    send_list = send_rows[0]
    peer_slots = send_list.shape[1]
    send_flat = send_list.reshape(-1)
    pick = (send_flat[:, None] == jnp.arange(node_rows)[None, :]).astype(jnp.bfloat16)
    outgoing = jnp.dot(pick, features, preferred_element_type=jnp.float32).astype(jnp.bfloat16)
    outgoing = outgoing.reshape(peer_count, peer_slots, feat_width)
    incoming = lax.all_to_all(outgoing, "nodes", split_axis=0, concat_axis=0, tiled=True)
    halo_table = jnp.concatenate([features, incoming.reshape(-1, feat_width)], axis=0)
    table_rows = halo_table.shape[0]

    w_all = jnp.concatenate([w_query, w_key, w_value], axis=1)
    projected = jnp.dot(features, w_all, preferred_element_type=jnp.float32)
    exp_query = jnp.exp(projected[:, :feat_width]).reshape(node_rows, HEADS, HEAD_DIM)
    exp_key = jnp.exp(projected[:, feat_width : 2 * feat_width]).reshape(node_rows, HEADS, HEAD_DIM)
    values = projected[:, 2 * feat_width :].reshape(node_rows, HEADS, HEAD_DIM)
    kv_part = jnp.einsum("ihd,ihe->hde", exp_key, values, precision=precise)
    ks_part = jnp.sum(exp_key, axis=0)
    kv_size = kv_part.size
    summary = group_sum(jnp.concatenate([kv_part.reshape(-1), ks_part.reshape(-1)]))
    kv_sum = summary[:kv_size].reshape(kv_part.shape)
    ks_sum = summary[kv_size:].reshape(ks_part.shape)

    cot_half = cotangent.astype(jnp.bfloat16)
    basis_grad = jnp.einsum("me,bde->bmd", cot_half, bases, preferred_element_type=jnp.float32)
    rel_count = tile_src.shape[1]
    aggregate, edge_weights = graph_conv(
        rel_coef, tile_src[0], tile_dst[0], tile_count[0], halo_table, basis_count
    )
    table_grad = jnp.einsum(
        "bnk,bkd->nd",
        edge_weights,
        basis_grad,
        precision=three_pass,
        preferred_element_type=jnp.float32,
    )
    aggregate = aggregate.reshape(rel_count, node_rows, feat_width)
    basis_in = jnp.einsum("rb,rmd->bmd", rel_coef, aggregate, precision=precise).astype(
        jnp.bfloat16
    )
    conv_out = jnp.einsum("bmd,bde->me", basis_in, bases, preferred_element_type=jnp.float32)
    normalizer = jnp.einsum("ihd,hd->ih", exp_query, ks_sum, precision=precise)
    attended = (
        jnp.einsum("ihd,hde->ihe", exp_query, kv_sum, precision=precise) / normalizer[:, :, None]
    )
    layer_out = attended.reshape(node_rows, feat_width) + conv_out
    coef_part = jnp.sum(aggregate[:, None] * basis_grad[None], axis=(2, 3))

    grad_heads = cotangent.reshape(node_rows, HEADS, HEAD_DIM)
    num_grad = grad_heads / normalizer[:, :, None]
    den_grad = -jnp.sum(grad_heads * attended, axis=2) / normalizer
    dkv_part = jnp.einsum("ihd,ihe->hde", exp_query, num_grad, precision=precise)
    dks_part = jnp.einsum("ihd,ih->hd", exp_query, den_grad, precision=precise)
    dks_size = dks_part.size
    reduced = group_sum(
        jnp.concatenate([dkv_part.reshape(-1), dks_part.reshape(-1), coef_part.reshape(-1)])
    )
    dkv_sum = reduced[:kv_size].reshape(dkv_part.shape)
    dks_sum = reduced[kv_size : kv_size + dks_size].reshape(dks_part.shape)
    coef_flat = lax.optimization_barrier(reduced[kv_size + dks_size :])
    coef_sum = coef_flat.reshape(coef_part.shape)
    query_side = (
        jnp.einsum("ihe,hde->ihd", num_grad, kv_sum, precision=precise)
        + den_grad[:, :, None] * ks_sum[None]
    )
    key_side = jnp.einsum("ihe,hde->ihd", values, dkv_sum, precision=precise) + dks_sum[None]
    value_side = jnp.einsum("ihd,hde->ihe", exp_key, dkv_sum, precision=precise)
    proj_grad = jnp.concatenate(
        [
            (query_side * exp_query).reshape(node_rows, feat_width),
            (key_side * exp_key).reshape(node_rows, feat_width),
            value_side.reshape(node_rows, feat_width),
        ],
        axis=1,
    ).astype(jnp.bfloat16)
    grad_x = jnp.einsum("mc,dc->md", proj_grad, w_all, preferred_element_type=jnp.float32)
    returned = lax.all_to_all(
        table_grad[node_rows:].astype(jnp.bfloat16).reshape(peer_count, peer_slots, feat_width),
        "nodes",
        split_axis=0,
        concat_axis=0,
        tiled=True,
    )
    back_grad = jnp.einsum(
        "km,kd->md", pick, returned.reshape(-1, feat_width), preferred_element_type=jnp.float32
    )
    grad_x = grad_x + table_grad[:node_rows] + back_grad
    feat_part = jnp.einsum("mc,me->ce", features, proj_grad, preferred_element_type=jnp.float32)
    basis_part = jnp.einsum("bmc,me->cbe", basis_in, cot_half, preferred_element_type=jnp.float32)
    stacked = block_sum(jnp.concatenate([feat_part, basis_part.reshape(feat_width, -1)], axis=1))
    stacked = stacked * norm_scale
    query_grad = stacked[:, :feat_width]
    key_grad = stacked[:, feat_width : 2 * feat_width]
    value_grad = stacked[:, 2 * feat_width : 3 * feat_width]
    bases_grad = jnp.transpose(
        stacked[:, 3 * feat_width :].reshape(feat_width, basis_count, feat_width), (1, 0, 2)
    )
    coef_grad = coef_sum * norm_scale
    return (layer_out, grad_x, query_grad, key_grad, value_grad, bases_grad, coef_grad)


def solution(mesh):
    in_specs = (
        P(("outer", "nodes"), None),
        P(),
        P(),
        P(),
        P(),
        P(),
        P(("outer", "nodes"), None, None),
        P(("outer", "nodes"), None, None, None),
        P(("outer", "nodes"), None, None, None),
        P(("outer", "nodes"), None, None),
        P(("outer", "nodes"), None),
    )
    out_specs = (P(("outer", "nodes"), None), P(("outer", "nodes"), None), P(), P(), P(), P(), P())
    return jax.shard_map(
        per_device, mesh=mesh, in_specs=in_specs, out_specs=out_specs, check_vma=False
    )
```

```python
import math

import jax
import jax.numpy as jnp
from jax import lax
from jax.experimental import pallas as pl
from jax.experimental.pallas import tpu as pltpu
from jax.sharding import PartitionSpec as P

HEADS = 8
HEAD_DIM = 64
TILE = 128


precise = lax.Precision.HIGHEST
three_pass = lax.Precision.HIGH
NT = (((1,), (1,)), ((), ()))


def group_sum(flat):
    axes = ("outer", "nodes")
    devices = lax.axis_size("outer") * lax.axis_size("nodes")
    size = flat.shape[0]
    chunk = -(-size // (devices * 128)) * 128
    padded = jnp.pad(flat, (0, devices * chunk - size)).reshape(devices, chunk)
    received = lax.all_to_all(padded, axes, split_axis=0, concat_axis=0, tiled=True)
    mine = jnp.sum(received, axis=0, keepdims=True)
    spread = jnp.broadcast_to(mine, (devices, chunk))
    gathered = lax.all_to_all(spread, axes, split_axis=0, concat_axis=0, tiled=True)
    return gathered.reshape(-1)[:size]


def block_sum(rows):
    axes = ("outer", "nodes")
    devices = lax.axis_size("outer") * lax.axis_size("nodes")
    row_blocks, _, cols = rows.shape
    parts = devices // row_blocks
    width = cols // parts
    tiles = jnp.stack([rows[:, :, p * width : (p + 1) * width] for p in range(parts)], axis=1)
    tiles = tiles.reshape(devices, 8, width)
    received = lax.all_to_all(tiles, axes, split_axis=0, concat_axis=0, tiled=True)
    mine = jnp.sum(received, axis=0, keepdims=True).astype(jnp.bfloat16)
    spread = jnp.broadcast_to(mine, (devices, 8, width))
    gathered = lax.all_to_all(spread, axes, split_axis=0, concat_axis=0, tiled=True)
    gathered = gathered.astype(jnp.float32).reshape(row_blocks, parts, 8, width).transpose(0, 2, 1, 3)
    return gathered.reshape(row_blocks * 8, cols)


def graph_kernel(coef_ref, src_ref, dst_ref, cnt_ref, table_ref, agg_ref, wsum_ref):
    tile = pl.program_id(0)
    rel_count = src_ref.shape[0]
    table_rows = table_ref.shape[0]
    basis_count = wsum_ref.shape[0]
    row_iota = lax.broadcasted_iota(jnp.int32, (table_rows, TILE), 0)
    node_iota = lax.broadcasted_iota(jnp.int32, (TILE, TILE), 0)
    slot_iota = lax.broadcasted_iota(jnp.int32, (TILE, TILE), 1)
    ones = jnp.ones((8, TILE), jnp.bfloat16)
    weights = [jnp.zeros((table_rows, TILE), jnp.float32) for _ in range(basis_count)]
    for r in range(rel_count):
        src_row = src_ref[r, 0]
        dst_row = dst_ref[r, 0]
        live = slot_iota < cnt_ref[r, tile]
        dst_t = ((node_iota == dst_row) & live).astype(jnp.bfloat16)
        src_t = (row_iota == src_row).astype(jnp.bfloat16)
        counts = lax.dot_general(dst_t, src_t, NT, preferred_element_type=jnp.float32)
        counts_t = lax.dot_general(src_t, dst_t, NT, preferred_element_type=jnp.float32)
        deg_col = jnp.maximum(jnp.sum(dst_t.astype(jnp.float32), axis=1, keepdims=True), 1.0)
        deg_row = jnp.maximum(
            lax.dot_general(ones, dst_t, NT, preferred_element_type=jnp.float32)[0:1], 1.0
        )
        sums = jnp.dot(counts.astype(jnp.bfloat16), table_ref[...], preferred_element_type=jnp.float32)
        agg_ref[r, 0] = sums / deg_col
        for b in range(basis_count):
            weights[b] = weights[b] + counts_t * (coef_ref[r, b] / deg_row)
    for b in range(basis_count):
        wsum_ref[b] = weights[b]


def graph_conv(rel_coef, src, dst, cnt, table, basis_count):
    rel_count, tiles, slots = src.shape
    table_rows, width = table.shape
    src4 = src.reshape(rel_count, tiles, 1, slots)
    dst4 = dst.reshape(rel_count, tiles, 1, slots)
    return pl.pallas_call(
        graph_kernel,
        grid=(tiles,),
        in_specs=[
            pl.BlockSpec(memory_space=pltpu.SMEM),
            pl.BlockSpec((rel_count, 1, 1, slots), lambda t: (0, t, 0, 0)),
            pl.BlockSpec((rel_count, 1, 1, slots), lambda t: (0, t, 0, 0)),
            pl.BlockSpec(memory_space=pltpu.SMEM),
            pl.BlockSpec((table_rows, width), lambda t: (0, 0)),
        ],
        out_specs=[
            pl.BlockSpec((rel_count, 1, TILE, width), lambda t: (0, t, 0, 0)),
            pl.BlockSpec((basis_count, table_rows, TILE), lambda t: (0, 0, t)),
        ],
        out_shape=[
            jax.ShapeDtypeStruct((rel_count, tiles, TILE, width), jnp.float32),
            jax.ShapeDtypeStruct((basis_count, table_rows, tiles * TILE), jnp.float32),
        ],
        compiler_params=pltpu.CompilerParams(
            dimension_semantics=("parallel",), vmem_limit_bytes=64 * 1024 * 1024
        ),
    )(rel_coef, src4, dst4, cnt, table)


def per_device(
    features,
    w_query,
    w_key,
    w_value,
    bases,
    rel_coef,
    send_rows,
    tile_src,
    tile_dst,
    tile_count,
    cotangent,
):
    node_rows, feat_width = features.shape
    peer_count = lax.axis_size("nodes")
    total_nodes = node_rows * peer_count * lax.axis_size("outer")
    norm_scale = 1.0 / math.sqrt(total_nodes)
    basis_count = bases.shape[0]
    send_list = send_rows[0]
    peer_slots = send_list.shape[1]
    send_flat = send_list.reshape(-1)
    pick = (send_flat[:, None] == jnp.arange(node_rows)[None, :]).astype(jnp.bfloat16)
    outgoing = jnp.dot(pick, features, preferred_element_type=jnp.float32).astype(jnp.bfloat16)
    outgoing = outgoing.reshape(peer_count, peer_slots, feat_width)
    incoming = lax.all_to_all(outgoing, "nodes", split_axis=0, concat_axis=0, tiled=True)
    halo_table = jnp.concatenate([features, incoming.reshape(-1, feat_width)], axis=0)
    table_rows = halo_table.shape[0]

    w_all = jnp.concatenate([w_query, w_key, w_value], axis=1)
    projected = jnp.dot(features, w_all, preferred_element_type=jnp.float32)
    exp_query = jnp.exp(projected[:, :feat_width]).reshape(node_rows, HEADS, HEAD_DIM)
    exp_key = jnp.exp(projected[:, feat_width : 2 * feat_width]).reshape(node_rows, HEADS, HEAD_DIM)
    values = projected[:, 2 * feat_width :].reshape(node_rows, HEADS, HEAD_DIM)
    kv_part = jnp.einsum("ihd,ihe->hde", exp_key, values, precision=precise)
    ks_part = jnp.sum(exp_key, axis=0)
    kv_size = kv_part.size
    summary = group_sum(jnp.concatenate([kv_part.reshape(-1), ks_part.reshape(-1)]))
    kv_sum = summary[:kv_size].reshape(kv_part.shape)
    ks_sum = summary[kv_size:].reshape(ks_part.shape)

    cot_half = cotangent.astype(jnp.bfloat16)
    basis_grad = jnp.einsum("me,bde->bmd", cot_half, bases, preferred_element_type=jnp.float32)
    rel_count = tile_src.shape[1]
    aggregate, edge_weights = graph_conv(
        rel_coef, tile_src[0], tile_dst[0], tile_count[0], halo_table, basis_count
    )
    table_grad = jnp.einsum(
        "bnk,bkd->nd",
        edge_weights,
        basis_grad,
        precision=three_pass,
        preferred_element_type=jnp.float32,
    )
    aggregate = aggregate.reshape(rel_count, node_rows, feat_width)
    basis_in = jnp.einsum("rb,rmd->bmd", rel_coef, aggregate, precision=precise).astype(
        jnp.bfloat16
    )
    conv_out = jnp.einsum("bmd,bde->me", basis_in, bases, preferred_element_type=jnp.float32)
    normalizer = jnp.einsum("ihd,hd->ih", exp_query, ks_sum, precision=precise)
    attended = (
        jnp.einsum("ihd,hde->ihe", exp_query, kv_sum, precision=precise) / normalizer[:, :, None]
    )
    layer_out = attended.reshape(node_rows, feat_width) + conv_out
    coef_part = jnp.sum(aggregate[:, None] * basis_grad[None], axis=(2, 3))

    grad_heads = cotangent.reshape(node_rows, HEADS, HEAD_DIM)
    num_grad = grad_heads / normalizer[:, :, None]
    den_grad = -jnp.sum(grad_heads * attended, axis=2) / normalizer
    dkv_part = jnp.einsum("ihd,ihe->hde", exp_query, num_grad, precision=precise)
    dks_part = jnp.einsum("ihd,ih->hd", exp_query, den_grad, precision=precise)
    dks_size = dks_part.size
    reduced = group_sum(
        jnp.concatenate([dkv_part.reshape(-1), dks_part.reshape(-1), coef_part.reshape(-1)])
    )
    dkv_sum = reduced[:kv_size].reshape(dkv_part.shape)
    dks_sum = reduced[kv_size : kv_size + dks_size].reshape(dks_part.shape)
    coef_flat = lax.optimization_barrier(reduced[kv_size + dks_size :])
    coef_sum = coef_flat.reshape(coef_part.shape)
    query_side = (
        jnp.einsum("ihe,hde->ihd", num_grad, kv_sum, precision=precise)
        + den_grad[:, :, None] * ks_sum[None]
    )
    key_side = jnp.einsum("ihe,hde->ihd", values, dkv_sum, precision=precise) + dks_sum[None]
    value_side = jnp.einsum("ihd,hde->ihe", exp_key, dkv_sum, precision=precise)
    proj_grad = jnp.concatenate(
        [
            (query_side * exp_query).reshape(node_rows, feat_width),
            (key_side * exp_key).reshape(node_rows, feat_width),
            value_side.reshape(node_rows, feat_width),
        ],
        axis=1,
    ).astype(jnp.bfloat16)
    grad_x = jnp.einsum("mc,dc->md", proj_grad, w_all, preferred_element_type=jnp.float32)
    returned = lax.all_to_all(
        table_grad[node_rows:].astype(jnp.bfloat16).reshape(peer_count, peer_slots, feat_width),
        "nodes",
        split_axis=0,
        concat_axis=0,
        tiled=True,
    )
    back_grad = jnp.einsum(
        "km,kd->md", pick, returned.reshape(-1, feat_width), preferred_element_type=jnp.float32
    )
    grad_x = grad_x + table_grad[:node_rows] + back_grad
    row_blocks = feat_width // 8
    feat_rows = jnp.einsum(
        "mrk,me->rke",
        features.reshape(node_rows, row_blocks, 8),
        proj_grad,
        preferred_element_type=jnp.float32,
    )
    basis_rows = jnp.einsum(
        "bmrk,me->rkbe",
        basis_in.reshape(basis_count, node_rows, row_blocks, 8),
        cot_half,
        preferred_element_type=jnp.float32,
    ).reshape(row_blocks, 8, basis_count * feat_width)
    rows = jnp.concatenate([feat_rows, basis_rows], axis=2)
    stacked = block_sum(rows)
    stacked = stacked * norm_scale
    query_grad = stacked[:, :feat_width]
    key_grad = stacked[:, feat_width : 2 * feat_width]
    value_grad = stacked[:, 2 * feat_width : 3 * feat_width]
    bases_grad = jnp.transpose(
        stacked[:, 3 * feat_width :].reshape(feat_width, basis_count, feat_width), (1, 0, 2)
    )
    coef_grad = coef_sum * norm_scale
    return (layer_out, grad_x, query_grad, key_grad, value_grad, bases_grad, coef_grad)


def solution(mesh):
    in_specs = (
        P(("outer", "nodes"), None),
        P(),
        P(),
        P(),
        P(),
        P(),
        P(("outer", "nodes"), None, None),
        P(("outer", "nodes"), None, None, None),
        P(("outer", "nodes"), None, None, None),
        P(("outer", "nodes"), None, None),
        P(("outer", "nodes"), None),
    )
    out_specs = (P(("outer", "nodes"), None), P(("outer", "nodes"), None), P(), P(), P(), P(), P())
    return jax.shard_map(
        per_device, mesh=mesh, in_specs=in_specs, out_specs=out_specs, check_vma=False
    )
```

```python
import math

import jax
import jax.numpy as jnp
from jax import lax
from jax.experimental import pallas as pl
from jax.experimental.pallas import tpu as pltpu
from jax.sharding import PartitionSpec as P

HEADS = 8
HEAD_DIM = 64
TILE = 128


precise = lax.Precision.HIGHEST
three_pass = lax.Precision.HIGH
NT = (((1,), (1,)), ((), ()))


def group_sum(flat):
    axes = ("outer", "nodes")
    devices = lax.axis_size("outer") * lax.axis_size("nodes")
    size = flat.shape[0]
    chunk = -(-size // (devices * 128)) * 128
    padded = jnp.pad(flat, (0, devices * chunk - size)).reshape(devices, chunk)
    received = lax.all_to_all(padded, axes, split_axis=0, concat_axis=0, tiled=True)
    mine = jnp.sum(received, axis=0, keepdims=True)
    spread = jnp.broadcast_to(mine, (devices, chunk))
    gathered = lax.all_to_all(spread, axes, split_axis=0, concat_axis=0, tiled=True)
    return gathered.reshape(-1)[:size]


def block_sum(rows):
    axes = ("outer", "nodes")
    devices = lax.axis_size("outer") * lax.axis_size("nodes")
    row_blocks, _, cols = rows.shape
    parts = devices // row_blocks
    width = cols // parts
    tiles = jnp.stack([rows[:, :, p * width : (p + 1) * width] for p in range(parts)], axis=1)
    tiles = tiles.reshape(devices, 8, width)
    received = lax.all_to_all(tiles, axes, split_axis=0, concat_axis=0, tiled=True)
    mine = jnp.sum(received, axis=0, keepdims=True).astype(jnp.bfloat16)
    spread = jnp.broadcast_to(mine, (devices, 8, width))
    gathered = lax.all_to_all(spread, axes, split_axis=0, concat_axis=0, tiled=True)
    gathered = gathered.astype(jnp.float32).reshape(row_blocks, parts, 8, width).transpose(0, 2, 1, 3)
    return gathered.reshape(row_blocks * 8, cols)


def graph_kernel(coef_ref, src_ref, dst_ref, cnt_ref, table_ref, agg_ref, wsum_ref):
    tile = pl.program_id(0)
    rel_count = src_ref.shape[0]
    table_rows = table_ref.shape[0]
    basis_count = wsum_ref.shape[0]
    row_iota = lax.broadcasted_iota(jnp.int32, (table_rows, TILE), 0)
    node_iota = lax.broadcasted_iota(jnp.int32, (TILE, TILE), 0)
    slot_iota = lax.broadcasted_iota(jnp.int32, (TILE, TILE), 1)
    ones = jnp.ones((8, TILE), jnp.bfloat16)
    weights = [jnp.zeros((table_rows, TILE), jnp.float32) for _ in range(basis_count)]
    for r in range(rel_count):
        src_row = src_ref[r, 0]
        dst_row = dst_ref[r, 0]
        live = slot_iota < cnt_ref[r, tile]
        dst_t = ((node_iota == dst_row) & live).astype(jnp.bfloat16)
        src_t = (row_iota == src_row).astype(jnp.bfloat16)
        counts = lax.dot_general(dst_t, src_t, NT, preferred_element_type=jnp.float32)
        counts_t = lax.dot_general(src_t, dst_t, NT, preferred_element_type=jnp.float32)
        deg_col = jnp.maximum(jnp.sum(dst_t.astype(jnp.float32), axis=1, keepdims=True), 1.0)
        deg_row = jnp.maximum(
            lax.dot_general(ones, dst_t, NT, preferred_element_type=jnp.float32)[0:1], 1.0
        )
        sums = jnp.dot(counts.astype(jnp.bfloat16), table_ref[...], preferred_element_type=jnp.float32)
        agg_ref[r, 0] = sums / deg_col
        for b in range(basis_count):
            weights[b] = weights[b] + counts_t * (coef_ref[r, b] / deg_row)
    for b in range(basis_count):
        wsum_ref[b] = weights[b]


def graph_conv(rel_coef, src, dst, cnt, table, basis_count):
    rel_count, tiles, slots = src.shape
    table_rows, width = table.shape
    src4 = src.reshape(rel_count, tiles, 1, slots)
    dst4 = dst.reshape(rel_count, tiles, 1, slots)
    return pl.pallas_call(
        graph_kernel,
        grid=(tiles,),
        in_specs=[
            pl.BlockSpec(memory_space=pltpu.SMEM),
            pl.BlockSpec((rel_count, 1, 1, slots), lambda t: (0, t, 0, 0)),
            pl.BlockSpec((rel_count, 1, 1, slots), lambda t: (0, t, 0, 0)),
            pl.BlockSpec(memory_space=pltpu.SMEM),
            pl.BlockSpec((table_rows, width), lambda t: (0, 0)),
        ],
        out_specs=[
            pl.BlockSpec((rel_count, 1, TILE, width), lambda t: (0, t, 0, 0)),
            pl.BlockSpec((basis_count, table_rows, TILE), lambda t: (0, 0, t)),
        ],
        out_shape=[
            jax.ShapeDtypeStruct((rel_count, tiles, TILE, width), jnp.float32),
            jax.ShapeDtypeStruct((basis_count, table_rows, tiles * TILE), jnp.float32),
        ],
        compiler_params=pltpu.CompilerParams(
            dimension_semantics=("parallel",), vmem_limit_bytes=64 * 1024 * 1024
        ),
    )(rel_coef, src4, dst4, cnt, table)


def per_device(
    features,
    w_query,
    w_key,
    w_value,
    bases,
    rel_coef,
    send_rows,
    tile_src,
    tile_dst,
    tile_count,
    cotangent,
):
    node_rows, feat_width = features.shape
    peer_count = lax.axis_size("nodes")
    total_nodes = node_rows * peer_count * lax.axis_size("outer")
    norm_scale = 1.0 / math.sqrt(total_nodes)
    basis_count = bases.shape[0]
    send_list = send_rows[0]
    peer_slots = send_list.shape[1]
    send_flat = send_list.reshape(-1)
    pick = (send_flat[:, None] == jnp.arange(node_rows)[None, :]).astype(jnp.bfloat16)
    outgoing = jnp.dot(pick, features, preferred_element_type=jnp.float32).astype(jnp.bfloat16)
    outgoing = outgoing.reshape(peer_count, peer_slots, feat_width)
    incoming = lax.all_to_all(outgoing, "nodes", split_axis=0, concat_axis=0, tiled=True)
    halo_table = jnp.concatenate([features, incoming.reshape(-1, feat_width)], axis=0)
    table_rows = halo_table.shape[0]

    w_all = jnp.concatenate([w_query, w_key, w_value], axis=1)
    projected = jnp.dot(features, w_all, preferred_element_type=jnp.float32)
    exp_query = jnp.exp(projected[:, :feat_width]).reshape(node_rows, HEADS, HEAD_DIM)
    exp_key = jnp.exp(projected[:, feat_width : 2 * feat_width]).reshape(node_rows, HEADS, HEAD_DIM)
    values = projected[:, 2 * feat_width :].reshape(node_rows, HEADS, HEAD_DIM)
    kv_part = jnp.einsum("ihd,ihe->hde", exp_key, values, precision=precise)
    ks_part = jnp.sum(exp_key, axis=0)
    kv_size = kv_part.size
    summary = group_sum(jnp.concatenate([kv_part.reshape(-1), ks_part.reshape(-1)]))
    kv_sum = summary[:kv_size].reshape(kv_part.shape)
    ks_sum = summary[kv_size:].reshape(ks_part.shape)

    cot_half = cotangent.astype(jnp.bfloat16)
    basis_grad = jnp.einsum("me,bde->bmd", cot_half, bases, preferred_element_type=jnp.float32)
    rel_count = tile_src.shape[1]
    aggregate, edge_weights = graph_conv(
        rel_coef, tile_src[0], tile_dst[0], tile_count[0], halo_table, basis_count
    )
    table_grad = jnp.einsum(
        "bnk,bkd->nd",
        edge_weights,
        basis_grad,
        precision=three_pass,
        preferred_element_type=jnp.float32,
    )
    aggregate = aggregate.reshape(rel_count, node_rows, feat_width)
    basis_in = jnp.einsum("rb,rmd->bmd", rel_coef, aggregate, precision=precise).astype(
        jnp.bfloat16
    )
    conv_out = jnp.einsum("bmd,bde->me", basis_in, bases, preferred_element_type=jnp.float32)
    normalizer = jnp.einsum("ihd,hd->ih", exp_query, ks_sum, precision=precise)
    attended = (
        jnp.einsum("ihd,hde->ihe", exp_query, kv_sum, precision=precise) / normalizer[:, :, None]
    )
    layer_out = attended.reshape(node_rows, feat_width) + conv_out
    coef_part = jnp.sum(aggregate[:, None] * basis_grad[None], axis=(2, 3))

    grad_heads = cotangent.reshape(node_rows, HEADS, HEAD_DIM)
    num_grad = grad_heads / normalizer[:, :, None]
    den_grad = -jnp.sum(grad_heads * attended, axis=2) / normalizer
    dkv_part = jnp.einsum("ihd,ihe->hde", exp_query, num_grad, precision=precise)
    dks_part = jnp.einsum("ihd,ih->hd", exp_query, den_grad, precision=precise)
    dks_size = dks_part.size
    reduced = group_sum(
        jnp.concatenate([dkv_part.reshape(-1), dks_part.reshape(-1)])
    )
    dkv_sum = reduced[:kv_size].reshape(dkv_part.shape)
    dks_sum = reduced[kv_size : kv_size + dks_size].reshape(dks_part.shape)
    query_side = (
        jnp.einsum("ihe,hde->ihd", num_grad, kv_sum, precision=precise)
        + den_grad[:, :, None] * ks_sum[None]
    )
    key_side = jnp.einsum("ihe,hde->ihd", values, dkv_sum, precision=precise) + dks_sum[None]
    value_side = jnp.einsum("ihd,hde->ihe", exp_key, dkv_sum, precision=precise)
    proj_grad = jnp.concatenate(
        [
            (query_side * exp_query).reshape(node_rows, feat_width),
            (key_side * exp_key).reshape(node_rows, feat_width),
            value_side.reshape(node_rows, feat_width),
        ],
        axis=1,
    ).astype(jnp.bfloat16)
    grad_x = jnp.einsum("mc,dc->md", proj_grad, w_all, preferred_element_type=jnp.float32)
    returned = lax.all_to_all(
        table_grad[node_rows:].astype(jnp.bfloat16).reshape(peer_count, peer_slots, feat_width),
        "nodes",
        split_axis=0,
        concat_axis=0,
        tiled=True,
    )
    back_grad = jnp.einsum(
        "km,kd->md", pick, returned.reshape(-1, feat_width), preferred_element_type=jnp.float32
    )
    grad_x = grad_x + table_grad[:node_rows] + back_grad
    row_blocks = feat_width // 8
    feat_rows = jnp.einsum(
        "mrk,me->rke",
        features.reshape(node_rows, row_blocks, 8),
        proj_grad,
        preferred_element_type=jnp.float32,
    )
    basis_rows = jnp.einsum(
        "bmrk,me->rkbe",
        basis_in.reshape(basis_count, node_rows, row_blocks, 8),
        cot_half,
        preferred_element_type=jnp.float32,
    ).reshape(row_blocks, 8, basis_count * feat_width)
    coef_cols = jnp.pad(
        coef_part.reshape(1, 1, -1), ((0, row_blocks - 1), (0, 7), (0, 256 - coef_part.size))
    )
    rows = jnp.concatenate([feat_rows, basis_rows, coef_cols], axis=2)
    stacked = block_sum(rows)
    stacked = stacked * norm_scale
    query_grad = stacked[:, :feat_width]
    key_grad = stacked[:, feat_width : 2 * feat_width]
    value_grad = stacked[:, 2 * feat_width : 3 * feat_width]
    bases_grad = jnp.transpose(
        stacked[:, 3 * feat_width : (3 + basis_count) * feat_width].reshape(
            feat_width, basis_count, feat_width
        ),
        (1, 0, 2),
    )
    coef_start = (3 + basis_count) * feat_width
    coef_grad = stacked[0, coef_start : coef_start + coef_part.size].reshape(coef_part.shape)
    return (layer_out, grad_x, query_grad, key_grad, value_grad, bases_grad, coef_grad)


def solution(mesh):
    in_specs = (
        P(("outer", "nodes"), None),
        P(),
        P(),
        P(),
        P(),
        P(),
        P(("outer", "nodes"), None, None),
        P(("outer", "nodes"), None, None, None),
        P(("outer", "nodes"), None, None, None),
        P(("outer", "nodes"), None, None),
        P(("outer", "nodes"), None),
    )
    out_specs = (P(("outer", "nodes"), None), P(("outer", "nodes"), None), P(), P(), P(), P(), P())
    return jax.shard_map(
        per_device, mesh=mesh, in_specs=in_specs, out_specs=out_specs, check_vma=False
    )
```

```python
import math

import jax
import jax.numpy as jnp
from jax import lax
from jax.experimental import pallas as pl
from jax.experimental.pallas import tpu as pltpu
from jax.sharding import PartitionSpec as P

HEADS = 8
HEAD_DIM = 64
TILE = 128


precise = lax.Precision.HIGHEST
three_pass = lax.Precision.HIGH
NT = (((1,), (1,)), ((), ()))


def group_sum(flat):
    axes = ("outer", "nodes")
    devices = lax.axis_size("outer") * lax.axis_size("nodes")
    size = flat.shape[0]
    chunk = -(-size // (devices * 128)) * 128
    padded = jnp.pad(flat, (0, devices * chunk - size)).reshape(devices, chunk)
    received = lax.all_to_all(padded, axes, split_axis=0, concat_axis=0, tiled=True)
    mine = jnp.sum(received, axis=0, keepdims=True)
    spread = jnp.broadcast_to(mine, (devices, chunk))
    gathered = lax.all_to_all(spread, axes, split_axis=0, concat_axis=0, tiled=True)
    return gathered.reshape(-1)[:size]


def block_sum(rows):
    axes = ("outer", "nodes")
    devices = lax.axis_size("outer") * lax.axis_size("nodes")
    row_blocks, _, cols = rows.shape
    parts = devices // row_blocks
    width = cols // parts
    tiles = jnp.stack([rows[:, :, p * width : (p + 1) * width] for p in range(parts)], axis=1)
    tiles = tiles.reshape(devices, 8, width)
    received = lax.all_to_all(tiles, axes, split_axis=0, concat_axis=0, tiled=True)
    mine = jnp.sum(received, axis=0, keepdims=True).astype(jnp.bfloat16)
    spread = jnp.broadcast_to(mine, (devices, 8, width))
    gathered = lax.all_to_all(spread, axes, split_axis=0, concat_axis=0, tiled=True)
    gathered = gathered.astype(jnp.float32).reshape(row_blocks, parts, 8, width).transpose(0, 2, 1, 3)
    return gathered.reshape(row_blocks * 8, cols)


def graph_kernel(coef_ref, src_ref, dst_ref, cnt_ref, table_ref, agg_ref, wsum_ref):
    tile = pl.program_id(0)
    rel_count = src_ref.shape[0]
    table_rows = table_ref.shape[0]
    basis_count = wsum_ref.shape[0]
    row_iota = lax.broadcasted_iota(jnp.int32, (table_rows, TILE), 0)
    node_iota = lax.broadcasted_iota(jnp.int32, (TILE, TILE), 0)
    slot_iota = lax.broadcasted_iota(jnp.int32, (TILE, TILE), 1)
    ones = jnp.ones((8, TILE), jnp.bfloat16)
    weights = [jnp.zeros((table_rows, TILE), jnp.float32) for _ in range(basis_count)]
    for r in range(rel_count):
        src_row = src_ref[r, 0]
        dst_row = dst_ref[r, 0]
        live = slot_iota < cnt_ref[r, tile]
        dst_t = ((node_iota == dst_row) & live).astype(jnp.bfloat16)
        src_t = (row_iota == src_row).astype(jnp.bfloat16)
        counts = lax.dot_general(dst_t, src_t, NT, preferred_element_type=jnp.float32)
        counts_t = lax.dot_general(src_t, dst_t, NT, preferred_element_type=jnp.float32)
        deg_col = jnp.maximum(jnp.sum(dst_t.astype(jnp.float32), axis=1, keepdims=True), 1.0)
        deg_row = jnp.maximum(
            lax.dot_general(ones, dst_t, NT, preferred_element_type=jnp.float32)[0:1], 1.0
        )
        sums = jnp.dot(counts.astype(jnp.bfloat16), table_ref[...], preferred_element_type=jnp.float32)
        agg_ref[r, 0] = sums / deg_col
        for b in range(basis_count):
            weights[b] = weights[b] + counts_t * (coef_ref[r, b] / deg_row)
    for b in range(basis_count):
        wsum_ref[b] = weights[b]


def graph_conv(rel_coef, src, dst, cnt, table, basis_count):
    rel_count, tiles, slots = src.shape
    table_rows, width = table.shape
    src4 = src.reshape(rel_count, tiles, 1, slots)
    dst4 = dst.reshape(rel_count, tiles, 1, slots)
    return pl.pallas_call(
        graph_kernel,
        grid=(tiles,),
        in_specs=[
            pl.BlockSpec(memory_space=pltpu.SMEM),
            pl.BlockSpec((rel_count, 1, 1, slots), lambda t: (0, t, 0, 0)),
            pl.BlockSpec((rel_count, 1, 1, slots), lambda t: (0, t, 0, 0)),
            pl.BlockSpec(memory_space=pltpu.SMEM),
            pl.BlockSpec((table_rows, width), lambda t: (0, 0)),
        ],
        out_specs=[
            pl.BlockSpec((rel_count, 1, TILE, width), lambda t: (0, t, 0, 0)),
            pl.BlockSpec((basis_count, table_rows, TILE), lambda t: (0, 0, t)),
        ],
        out_shape=[
            jax.ShapeDtypeStruct((rel_count, tiles, TILE, width), jnp.float32),
            jax.ShapeDtypeStruct((basis_count, table_rows, tiles * TILE), jnp.float32),
        ],
        compiler_params=pltpu.CompilerParams(
            dimension_semantics=("parallel",), vmem_limit_bytes=64 * 1024 * 1024
        ),
    )(rel_coef, src4, dst4, cnt, table)


def per_device(
    features,
    w_query,
    w_key,
    w_value,
    bases,
    rel_coef,
    send_rows,
    tile_src,
    tile_dst,
    tile_count,
    cotangent,
):
    node_rows, feat_width = features.shape
    peer_count = lax.axis_size("nodes")
    total_nodes = node_rows * peer_count * lax.axis_size("outer")
    norm_scale = 1.0 / math.sqrt(total_nodes)
    basis_count = bases.shape[0]
    send_list = send_rows[0]
    peer_slots = send_list.shape[1]
    send_flat = send_list.reshape(-1)
    pick = (send_flat[:, None] == jnp.arange(node_rows)[None, :]).astype(jnp.bfloat16)
    outgoing = jnp.dot(pick, features, preferred_element_type=jnp.float32).astype(jnp.bfloat16)
    outgoing = outgoing.reshape(peer_count, peer_slots, feat_width)
    incoming = lax.all_to_all(outgoing, "nodes", split_axis=0, concat_axis=0, tiled=True)
    halo_table = jnp.concatenate([features, incoming.reshape(-1, feat_width)], axis=0)
    table_rows = halo_table.shape[0]

    w_all = jnp.concatenate([w_query, w_key, w_value], axis=1)
    projected = jnp.dot(features, w_all, preferred_element_type=jnp.float32)
    exp_query = jnp.exp(projected[:, :feat_width]).reshape(node_rows, HEADS, HEAD_DIM)
    exp_key = jnp.exp(projected[:, feat_width : 2 * feat_width]).reshape(node_rows, HEADS, HEAD_DIM)
    values = projected[:, 2 * feat_width :].reshape(node_rows, HEADS, HEAD_DIM)
    kv_part = jnp.einsum("ihd,ihe->hde", exp_key, values, precision=precise)
    ks_part = jnp.sum(exp_key, axis=0)
    kv_size = kv_part.size
    summary_part, halo_table = lax.optimization_barrier(
        (jnp.concatenate([kv_part.reshape(-1), ks_part.reshape(-1)]), halo_table)
    )
    summary = group_sum(summary_part)
    kv_sum = summary[:kv_size].reshape(kv_part.shape)
    ks_sum = summary[kv_size:].reshape(ks_part.shape)

    cot_half = cotangent.astype(jnp.bfloat16)
    basis_grad = jnp.einsum("me,bde->bmd", cot_half, bases, preferred_element_type=jnp.float32)
    rel_count = tile_src.shape[1]
    aggregate, edge_weights = graph_conv(
        rel_coef, tile_src[0], tile_dst[0], tile_count[0], halo_table, basis_count
    )
    table_grad = jnp.einsum(
        "bnk,bkd->nd",
        edge_weights,
        basis_grad,
        precision=three_pass,
        preferred_element_type=jnp.float32,
    )
    aggregate = aggregate.reshape(rel_count, node_rows, feat_width)
    basis_in = jnp.einsum("rb,rmd->bmd", rel_coef, aggregate, precision=precise).astype(
        jnp.bfloat16
    )
    conv_out = jnp.einsum("bmd,bde->me", basis_in, bases, preferred_element_type=jnp.float32)
    normalizer = jnp.einsum("ihd,hd->ih", exp_query, ks_sum, precision=precise)
    attended = (
        jnp.einsum("ihd,hde->ihe", exp_query, kv_sum, precision=precise) / normalizer[:, :, None]
    )
    layer_out = attended.reshape(node_rows, feat_width) + conv_out
    coef_part = jnp.sum(aggregate[:, None] * basis_grad[None], axis=(2, 3))

    grad_heads = cotangent.reshape(node_rows, HEADS, HEAD_DIM)
    num_grad = grad_heads / normalizer[:, :, None]
    den_grad = -jnp.sum(grad_heads * attended, axis=2) / normalizer
    dkv_part = jnp.einsum("ihd,ihe->hde", exp_query, num_grad, precision=precise)
    dks_part = jnp.einsum("ihd,ih->hd", exp_query, den_grad, precision=precise)
    dks_size = dks_part.size
    reduced = group_sum(
        jnp.concatenate([dkv_part.reshape(-1), dks_part.reshape(-1)])
    )
    dkv_sum = reduced[:kv_size].reshape(dkv_part.shape)
    dks_sum = reduced[kv_size : kv_size + dks_size].reshape(dks_part.shape)
    query_side = (
        jnp.einsum("ihe,hde->ihd", num_grad, kv_sum, precision=precise)
        + den_grad[:, :, None] * ks_sum[None]
    )
    key_side = jnp.einsum("ihe,hde->ihd", values, dkv_sum, precision=precise) + dks_sum[None]
    value_side = jnp.einsum("ihd,hde->ihe", exp_key, dkv_sum, precision=precise)
    proj_grad = jnp.concatenate(
        [
            (query_side * exp_query).reshape(node_rows, feat_width),
            (key_side * exp_key).reshape(node_rows, feat_width),
            value_side.reshape(node_rows, feat_width),
        ],
        axis=1,
    ).astype(jnp.bfloat16)
    grad_x = jnp.einsum("mc,dc->md", proj_grad, w_all, preferred_element_type=jnp.float32)
    returned = lax.all_to_all(
        table_grad[node_rows:].astype(jnp.bfloat16).reshape(peer_count, peer_slots, feat_width),
        "nodes",
        split_axis=0,
        concat_axis=0,
        tiled=True,
    )
    back_grad = jnp.einsum(
        "km,kd->md", pick, returned.reshape(-1, feat_width), preferred_element_type=jnp.float32
    )
    grad_x = grad_x + table_grad[:node_rows] + back_grad
    row_blocks = feat_width // 8
    feat_rows = jnp.einsum(
        "mrk,me->rke",
        features.reshape(node_rows, row_blocks, 8),
        proj_grad,
        preferred_element_type=jnp.float32,
    )
    basis_rows = jnp.einsum(
        "bmrk,me->rkbe",
        basis_in.reshape(basis_count, node_rows, row_blocks, 8),
        cot_half,
        preferred_element_type=jnp.float32,
    ).reshape(row_blocks, 8, basis_count * feat_width)
    coef_cols = jnp.pad(
        coef_part.reshape(1, 1, -1), ((0, row_blocks - 1), (0, 7), (0, 256 - coef_part.size))
    )
    rows = jnp.concatenate([feat_rows, basis_rows, coef_cols], axis=2)
    stacked = block_sum(rows)
    stacked = stacked * norm_scale
    query_grad = stacked[:, :feat_width]
    key_grad = stacked[:, feat_width : 2 * feat_width]
    value_grad = stacked[:, 2 * feat_width : 3 * feat_width]
    bases_grad = jnp.transpose(
        stacked[:, 3 * feat_width : (3 + basis_count) * feat_width].reshape(
            feat_width, basis_count, feat_width
        ),
        (1, 0, 2),
    )
    coef_start = (3 + basis_count) * feat_width
    coef_grad = stacked[0, coef_start : coef_start + coef_part.size].reshape(coef_part.shape)
    return (layer_out, grad_x, query_grad, key_grad, value_grad, bases_grad, coef_grad)


def solution(mesh):
    in_specs = (
        P(("outer", "nodes"), None),
        P(),
        P(),
        P(),
        P(),
        P(),
        P(("outer", "nodes"), None, None),
        P(("outer", "nodes"), None, None, None),
        P(("outer", "nodes"), None, None, None),
        P(("outer", "nodes"), None, None),
        P(("outer", "nodes"), None),
    )
    out_specs = (P(("outer", "nodes"), None), P(("outer", "nodes"), None), P(), P(), P(), P(), P())
    return jax.shard_map(
        per_device, mesh=mesh, in_specs=in_specs, out_specs=out_specs, check_vma=False
    )
```

```python
import math

import jax
import jax.numpy as jnp
from jax import lax
from jax.experimental import pallas as pl
from jax.experimental.pallas import tpu as pltpu
from jax.sharding import PartitionSpec as P

HEADS = 8
HEAD_DIM = 64
TILE = 128


precise = lax.Precision.HIGHEST
three_pass = lax.Precision.HIGH
NT = (((1,), (1,)), ((), ()))


def group_sum(flat):
    axes = ("outer", "nodes")
    devices = lax.axis_size("outer") * lax.axis_size("nodes")
    size = flat.shape[0]
    chunk = -(-size // (devices * 1024)) * 1024
    padded = jnp.pad(flat, (0, devices * chunk - size)).reshape(devices, chunk // 128, 128)
    received = lax.all_to_all(padded, axes, split_axis=0, concat_axis=0, tiled=True)
    mine = jnp.sum(received, axis=0, keepdims=True)
    spread = jnp.broadcast_to(mine, (devices, chunk // 128, 128))
    gathered = lax.all_to_all(spread, axes, split_axis=0, concat_axis=0, tiled=True)
    return gathered.reshape(-1)[:size]


def block_sum(rows):
    axes = ("outer", "nodes")
    devices = lax.axis_size("outer") * lax.axis_size("nodes")
    row_blocks, _, cols = rows.shape
    parts = devices // row_blocks
    width = cols // parts
    tiles = jnp.stack([rows[:, :, p * width : (p + 1) * width] for p in range(parts)], axis=1)
    tiles = tiles.reshape(devices, 8, width)
    received = lax.all_to_all(tiles, axes, split_axis=0, concat_axis=0, tiled=True)
    mine = jnp.sum(received, axis=0, keepdims=True).astype(jnp.bfloat16)
    spread = jnp.broadcast_to(mine, (devices, 8, width))
    gathered = lax.all_to_all(spread, axes, split_axis=0, concat_axis=0, tiled=True)
    gathered = gathered.astype(jnp.float32).reshape(row_blocks, parts, 8, width).transpose(0, 2, 1, 3)
    return gathered.reshape(row_blocks * 8, cols)


def graph_kernel(coef_ref, src_ref, dst_ref, cnt_ref, table_ref, agg_ref, wsum_ref):
    tile = pl.program_id(0)
    rel_count = src_ref.shape[0]
    table_rows = table_ref.shape[0]
    basis_count = wsum_ref.shape[0]
    row_iota = lax.broadcasted_iota(jnp.int32, (table_rows, TILE), 0)
    node_iota = lax.broadcasted_iota(jnp.int32, (TILE, TILE), 0)
    slot_iota = lax.broadcasted_iota(jnp.int32, (TILE, TILE), 1)
    ones = jnp.ones((8, TILE), jnp.bfloat16)
    weights = [jnp.zeros((table_rows, TILE), jnp.float32) for _ in range(basis_count)]
    for r in range(rel_count):
        src_row = src_ref[r, 0]
        dst_row = dst_ref[r, 0]
        live = slot_iota < cnt_ref[r, tile]
        dst_t = ((node_iota == dst_row) & live).astype(jnp.bfloat16)
        src_t = (row_iota == src_row).astype(jnp.bfloat16)
        counts = lax.dot_general(dst_t, src_t, NT, preferred_element_type=jnp.float32)
        counts_t = lax.dot_general(src_t, dst_t, NT, preferred_element_type=jnp.float32)
        deg_col = jnp.maximum(jnp.sum(dst_t.astype(jnp.float32), axis=1, keepdims=True), 1.0)
        deg_row = jnp.maximum(
            lax.dot_general(ones, dst_t, NT, preferred_element_type=jnp.float32)[0:1], 1.0
        )
        sums = jnp.dot(counts.astype(jnp.bfloat16), table_ref[...], preferred_element_type=jnp.float32)
        agg_ref[r, 0] = sums / deg_col
        for b in range(basis_count):
            weights[b] = weights[b] + counts_t * (coef_ref[r, b] / deg_row)
    for b in range(basis_count):
        wsum_ref[b] = weights[b]


def graph_conv(rel_coef, src, dst, cnt, table, basis_count):
    rel_count, tiles, slots = src.shape
    table_rows, width = table.shape
    src4 = src.reshape(rel_count, tiles, 1, slots)
    dst4 = dst.reshape(rel_count, tiles, 1, slots)
    return pl.pallas_call(
        graph_kernel,
        grid=(tiles,),
        in_specs=[
            pl.BlockSpec(memory_space=pltpu.SMEM),
            pl.BlockSpec((rel_count, 1, 1, slots), lambda t: (0, t, 0, 0)),
            pl.BlockSpec((rel_count, 1, 1, slots), lambda t: (0, t, 0, 0)),
            pl.BlockSpec(memory_space=pltpu.SMEM),
            pl.BlockSpec((table_rows, width), lambda t: (0, 0)),
        ],
        out_specs=[
            pl.BlockSpec((rel_count, 1, TILE, width), lambda t: (0, t, 0, 0)),
            pl.BlockSpec((basis_count, table_rows, TILE), lambda t: (0, 0, t)),
        ],
        out_shape=[
            jax.ShapeDtypeStruct((rel_count, tiles, TILE, width), jnp.float32),
            jax.ShapeDtypeStruct((basis_count, table_rows, tiles * TILE), jnp.float32),
        ],
        compiler_params=pltpu.CompilerParams(
            dimension_semantics=("parallel",), vmem_limit_bytes=64 * 1024 * 1024
        ),
    )(rel_coef, src4, dst4, cnt, table)


def per_device(
    features,
    w_query,
    w_key,
    w_value,
    bases,
    rel_coef,
    send_rows,
    tile_src,
    tile_dst,
    tile_count,
    cotangent,
):
    node_rows, feat_width = features.shape
    peer_count = lax.axis_size("nodes")
    total_nodes = node_rows * peer_count * lax.axis_size("outer")
    norm_scale = 1.0 / math.sqrt(total_nodes)
    basis_count = bases.shape[0]
    send_list = send_rows[0]
    peer_slots = send_list.shape[1]
    send_flat = send_list.reshape(-1)
    pick = (send_flat[:, None] == jnp.arange(node_rows)[None, :]).astype(jnp.bfloat16)
    outgoing = jnp.dot(pick, features, preferred_element_type=jnp.float32).astype(jnp.bfloat16)
    outgoing = outgoing.reshape(peer_count, peer_slots, feat_width)
    incoming = lax.all_to_all(outgoing, "nodes", split_axis=0, concat_axis=0, tiled=True)
    halo_table = jnp.concatenate([features, incoming.reshape(-1, feat_width)], axis=0)
    table_rows = halo_table.shape[0]

    w_all = jnp.concatenate([w_query, w_key, w_value], axis=1)
    projected = jnp.dot(features, w_all, preferred_element_type=jnp.float32)
    exp_query = jnp.exp(projected[:, :feat_width]).reshape(node_rows, HEADS, HEAD_DIM)
    exp_key = jnp.exp(projected[:, feat_width : 2 * feat_width]).reshape(node_rows, HEADS, HEAD_DIM)
    values = projected[:, 2 * feat_width :].reshape(node_rows, HEADS, HEAD_DIM)
    kv_part = jnp.einsum("ihd,ihe->hde", exp_key, values, precision=precise)
    ks_part = jnp.sum(exp_key, axis=0)
    kv_size = kv_part.size
    summary = group_sum(jnp.concatenate([kv_part.reshape(-1), ks_part.reshape(-1)]))
    kv_sum = summary[:kv_size].reshape(kv_part.shape)
    ks_sum = summary[kv_size:].reshape(ks_part.shape)

    cot_half = cotangent.astype(jnp.bfloat16)
    basis_grad = jnp.einsum("me,bde->bmd", cot_half, bases, preferred_element_type=jnp.float32)
    rel_count = tile_src.shape[1]
    aggregate, edge_weights = graph_conv(
        rel_coef, tile_src[0], tile_dst[0], tile_count[0], halo_table, basis_count
    )
    table_grad = jnp.einsum(
        "bnk,bkd->nd",
        edge_weights,
        basis_grad,
        precision=three_pass,
        preferred_element_type=jnp.float32,
    )
    aggregate = aggregate.reshape(rel_count, node_rows, feat_width)
    basis_in = jnp.einsum("rb,rmd->bmd", rel_coef, aggregate, precision=precise).astype(
        jnp.bfloat16
    )
    conv_out = jnp.einsum("bmd,bde->me", basis_in, bases, preferred_element_type=jnp.float32)
    normalizer = jnp.einsum("ihd,hd->ih", exp_query, ks_sum, precision=precise)
    attended = (
        jnp.einsum("ihd,hde->ihe", exp_query, kv_sum, precision=precise) / normalizer[:, :, None]
    )
    layer_out = attended.reshape(node_rows, feat_width) + conv_out
    coef_part = jnp.sum(aggregate[:, None] * basis_grad[None], axis=(2, 3))

    grad_heads = cotangent.reshape(node_rows, HEADS, HEAD_DIM)
    num_grad = grad_heads / normalizer[:, :, None]
    den_grad = -jnp.sum(grad_heads * attended, axis=2) / normalizer
    dkv_part = jnp.einsum("ihd,ihe->hde", exp_query, num_grad, precision=precise)
    dks_part = jnp.einsum("ihd,ih->hd", exp_query, den_grad, precision=precise)
    dks_size = dks_part.size
    reduced = group_sum(
        jnp.concatenate([dkv_part.reshape(-1), dks_part.reshape(-1), coef_part.reshape(-1)])
    )
    dkv_sum = reduced[:kv_size].reshape(dkv_part.shape)
    dks_sum = reduced[kv_size : kv_size + dks_size].reshape(dks_part.shape)
    coef_flat = lax.optimization_barrier(reduced[kv_size + dks_size :])
    coef_sum = coef_flat.reshape(coef_part.shape)
    query_side = (
        jnp.einsum("ihe,hde->ihd", num_grad, kv_sum, precision=precise)
        + den_grad[:, :, None] * ks_sum[None]
    )
    key_side = jnp.einsum("ihe,hde->ihd", values, dkv_sum, precision=precise) + dks_sum[None]
    value_side = jnp.einsum("ihd,hde->ihe", exp_key, dkv_sum, precision=precise)
    proj_grad = jnp.concatenate(
        [
            (query_side * exp_query).reshape(node_rows, feat_width),
            (key_side * exp_key).reshape(node_rows, feat_width),
            value_side.reshape(node_rows, feat_width),
        ],
        axis=1,
    ).astype(jnp.bfloat16)
    grad_x = jnp.einsum("mc,dc->md", proj_grad, w_all, preferred_element_type=jnp.float32)
    returned = lax.all_to_all(
        table_grad[node_rows:].astype(jnp.bfloat16).reshape(peer_count, peer_slots, feat_width),
        "nodes",
        split_axis=0,
        concat_axis=0,
        tiled=True,
    )
    back_grad = jnp.einsum(
        "km,kd->md", pick, returned.reshape(-1, feat_width), preferred_element_type=jnp.float32
    )
    grad_x = grad_x + table_grad[:node_rows] + back_grad
    row_blocks = feat_width // 8
    feat_rows = jnp.einsum(
        "mrk,me->rke",
        features.reshape(node_rows, row_blocks, 8),
        proj_grad,
        preferred_element_type=jnp.float32,
    )
    basis_rows = jnp.einsum(
        "bmrk,me->rkbe",
        basis_in.reshape(basis_count, node_rows, row_blocks, 8),
        cot_half,
        preferred_element_type=jnp.float32,
    ).reshape(row_blocks, 8, basis_count * feat_width)
    rows = jnp.concatenate([feat_rows, basis_rows], axis=2)
    stacked = block_sum(rows)
    stacked = stacked * norm_scale
    query_grad = stacked[:, :feat_width]
    key_grad = stacked[:, feat_width : 2 * feat_width]
    value_grad = stacked[:, 2 * feat_width : 3 * feat_width]
    bases_grad = jnp.transpose(
        stacked[:, 3 * feat_width :].reshape(feat_width, basis_count, feat_width), (1, 0, 2)
    )
    coef_grad = coef_sum * norm_scale
    return (layer_out, grad_x, query_grad, key_grad, value_grad, bases_grad, coef_grad)


def solution(mesh):
    in_specs = (
        P(("outer", "nodes"), None),
        P(),
        P(),
        P(),
        P(),
        P(),
        P(("outer", "nodes"), None, None),
        P(("outer", "nodes"), None, None, None),
        P(("outer", "nodes"), None, None, None),
        P(("outer", "nodes"), None, None),
        P(("outer", "nodes"), None),
    )
    out_specs = (P(("outer", "nodes"), None), P(("outer", "nodes"), None), P(), P(), P(), P(), P())
    return jax.shard_map(
        per_device, mesh=mesh, in_specs=in_specs, out_specs=out_specs, check_vma=False
    )
```
